32 devices in a mesh: grp: 2 (over y), blk: 4 (over z), head: 2 (over x), sub: 2 (over core).
Axes of the slice: x: 2, y: 2, z: 4, core: 2. Of those that a mesh axis runs over, the one named last changes fastest.
Arguments:
- queries: bfloat16 [4096, 4096], P(('grp', 'blk', 'head', 'sub')), parts along dimension 0, may hold values from -46 to 46
- keys: bfloat16 [4096, 4096], P(('grp', 'blk', 'head', 'sub')), parts along dimension 0, may hold values from -4 to 4
- values: bfloat16 [4096, 4096], P(('grp', 'blk', 'head', 'sub')), parts along dimension 0, may hold values from -6 to 6
- block_lists: int32 [32, 16, 8], replicated, may hold values from 0 to 15, as said below
Outputs:
- attended: bfloat16 [4096, 4096], P(('grp', 'blk', 'head', 'sub')), parts along dimension 0
The draws below stay inside these ranges and needn't reach their ends.
There are 2 independent parts, one for each index of `grp`. The reference program is written for one: setup_inputs(seed, part) draws one part's arguments, and reference() takes and returns one part's arrays. A program takes and returns all parts, laid end to end along the dimension named above; an argument that names none is the same for every part. Nothing has to cross between parts.
Inputs may be any that keep to these rules, and one draw needn't show every extreme that they name: `block_lists`: the first entry of every list is the query tile itself; entries may repeat. Tiles are numbered frame by frame, 4 to a frame. In each head either all entries lie in the query tile's frame or the frames next to it, or all entries have the query tile's position within its frame.
All inputs are finite; a program needn't handle non-finite values.
Results may differ from the reference program's by a relative error of at most 0.0065.
Values may be sent and summed in bfloat16 or wider, within the bound.
A program may use at most 64 MiB of HBM per device.

```python
import math
import jax
import jax.numpy as jnp
from jax import lax

HEADS = 32
HEAD_DIM = 128
TILE = 128
LIST = 8
FRAME_TILES = 4
SEQ = 2048
QTILES = 16


def draw_pair(key):
    col_count = HEADS * HEAD_DIM
    seed_query, seed_keys = jax.random.split(jax.random.fold_in(key, 11), 2)
    query_draw = jnp.clip(jax.random.normal(seed_query, (SEQ, col_count), jnp.float32), -4.0, 4.0)
    keys_draw = jnp.clip(jax.random.normal(seed_keys, (SEQ, col_count), jnp.float32), -4.0, 4.0)
    return (query_draw, keys_draw)


def draw_queries(key, part):
    query_draw, keys_draw = draw_pair(key)
    return query_draw.astype(jnp.bfloat16)


def draw_keys(key, part):
    query_draw, keys_draw = draw_pair(key)
    return keys_draw.astype(jnp.bfloat16)


def draw_block_lists(key, part):
    seed_one, seed_two, seed_three, seed_four = jax.random.split(jax.random.fold_in(key, 23), 4)
    frame_count = QTILES // FRAME_TILES
    shape_all = (HEADS, QTILES, LIST)
    pattern = jax.random.randint(seed_one, (HEADS, 1, 1), 0, 2)
    tile_index = jnp.arange(QTILES, dtype=jnp.int32)[None, :, None]
    frame_no = tile_index // FRAME_TILES
    slot_no = tile_index % FRAME_TILES
    frame_step = jax.random.randint(seed_two, shape_all, -1, 2)
    near_frame = jnp.clip(frame_no + frame_step, 0, frame_count - 1)
    near_slot = jax.random.randint(seed_three, shape_all, 0, FRAME_TILES)
    spatial_tile = near_frame * FRAME_TILES + near_slot
    far_frame = jax.random.randint(seed_four, shape_all, 0, frame_count)
    temporal_tile = far_frame * FRAME_TILES + slot_no
    chosen = jnp.where(pattern == 1, temporal_tile, spatial_tile)
    first_col = jnp.arange(LIST, dtype=jnp.int32)[None, None, :] == 0
    return jnp.where(first_col, tile_index, chosen).astype(jnp.int32)


def block_levels(stream_key, dims, shards, low, largest):
    factor_of = 1.0
    for position, shards_of in shards:
        heights = jax.random.uniform(jax.random.fold_in(jax.random.fold_in(stream_key, 6), position), (shards_of,), jnp.float32, low / len(shards), largest / len(shards))
        factor_of = factor_of * jnp.repeat(jnp.exp(heights), dims[position] // shards_of).reshape((-1,) + (1,) * (len(dims) - 1 - position))
    return factor_of


def gaussian(stream_key, extent, width, reach, cuts=(), kind=jnp.bfloat16):
    gain = block_levels(stream_key, extent, cuts, -0.22, 0.18) if cuts else 1.0
    result = jax.random.normal(stream_key, extent, jnp.float32) * width * gain
    return jnp.minimum(jnp.maximum(result, -reach), reach).astype(kind)


def setup_inputs(seed: int = 0, part: int = 0) -> dict:
    splits = jax.random.split(jax.random.key(seed), 5)
    part_splits = jax.random.split(jax.random.fold_in(splits[4], part), 5)
    return {
        "queries": draw_queries(jax.random.fold_in(jax.random.fold_in(splits[4], part), 71), part),
        "keys": draw_keys(jax.random.fold_in(jax.random.fold_in(splits[4], part), 71), part),
        "values": gaussian(part_splits[2], (SEQ, HEADS * HEAD_DIM), 1.0, 6.0, ((0, 16),)),
        "block_lists": draw_block_lists(jax.random.fold_in(splits[4], 71), part),
    }


def reference(queries, keys, values, block_lists):
    tile_ids = jnp.arange(QTILES, dtype=jnp.int32)
    tile_mask = jnp.any(block_lists[:, :, :, None] == tile_ids, axis=2)
    score_scale = 1.0 / math.sqrt(HEAD_DIM)

    def one_head(head_no):
        col_start = (head_no * HEAD_DIM).astype(jnp.int32)
        q_head = lax.dynamic_slice_in_dim(queries, col_start, HEAD_DIM, 1)
        k_head = lax.dynamic_slice_in_dim(keys, col_start, HEAD_DIM, 1)
        v_head = lax.dynamic_slice_in_dim(values, col_start, HEAD_DIM, 1)
        allowed = jnp.repeat(jnp.repeat(tile_mask[head_no], TILE, axis=0), TILE, axis=1)
        scores = jnp.dot(q_head, k_head.T, preferred_element_type=jnp.float32) * score_scale
        row_top = lax.optimization_barrier(jnp.max(jnp.where(allowed, scores, -jnp.inf), axis=1, keepdims=True))
        weights = jnp.where(allowed, jnp.exp(scores - row_top), 0.0)
        row_total = lax.optimization_barrier(jnp.sum(weights, axis=1, keepdims=True))
        numerator = jnp.dot(weights.astype(jnp.bfloat16), v_head, preferred_element_type=jnp.float32)
        return (numerator / row_total).astype(jnp.bfloat16)
    heads_out = lax.map(one_head, jnp.arange(HEADS, dtype=jnp.int32))
    return jnp.transpose(heads_out, (1, 0, 2)).reshape(SEQ, HEADS * HEAD_DIM)
```

```python
import functools
import math

import jax
import jax.numpy as jnp
from jax import lax
from jax.experimental import pallas as pl
from jax.experimental.pallas import tpu as pltpu
from jax.sharding import PartitionSpec as P

HEADS = 32
HEAD_DIM = 128
TILE = 128


NEG_FLOOR = -1e30


def query_rows(block_lists, first_head, heads_here, query_tokens):
    tile_ids = jnp.arange(block_lists.shape[1], dtype=jnp.int32)
    lists_local = lax.dynamic_slice_in_dim(block_lists, first_head, heads_here, 0)
    tile_mask = jnp.any(lists_local[:, :, :, None] == tile_ids, axis=2).astype(jnp.bfloat16)
    query_onehot = ((query_tokens // TILE)[:, None] == tile_ids[None, :]).astype(jnp.bfloat16)
    listed = jnp.einsum("qi,hij->hqj", query_onehot, tile_mask, preferred_element_type=jnp.float32)
    return listed.astype(jnp.bfloat16)


def attend_block(state_now, key_block, value_block, allowed, query_local, score_scale):
    top_old, total_old, accum_old = state_now
    scores = (
        jnp.einsum("qhd,khd->hqk", query_local, key_block, preferred_element_type=jnp.float32)
        * score_scale
    )
    top_new = jnp.maximum(top_old, jnp.max(jnp.where(allowed, scores, NEG_FLOOR), axis=2))
    factor = jnp.exp(top_old - top_new)
    weights = jnp.where(allowed, jnp.exp(scores - top_new[:, :, None]), 0.0)
    total_new = total_old * factor + jnp.sum(weights, axis=2)
    product = jnp.einsum(
        "hqk,khd->qhd",
        weights.astype(jnp.bfloat16),
        value_block,
        preferred_element_type=jnp.float32,
    )
    accum_new = accum_old * jnp.transpose(factor)[:, :, None] + product
    return (top_new, total_new, accum_new)


def make_step(query_local, listed_rows, key_token, block_len, tile_total):
    score_scale = 1.0 / math.sqrt(HEAD_DIM)
    tile_ids = jnp.arange(tile_total, dtype=jnp.int32)

    def fold_step(state_now, piece, first_row):
        key_piece, value_piece = piece
        block_count = key_piece.shape[0] // block_len

        def one_block(block_index, state_in):
            key_block = lax.dynamic_slice_in_dim(key_piece, block_index * block_len, block_len, 0)
            value_block = lax.dynamic_slice_in_dim(
                value_piece, block_index * block_len, block_len, 0
            )
            positions = block_index * block_len + jnp.arange(block_len, dtype=jnp.int32)
            key_tiles = key_token(positions) // TILE
            key_onehot = (tile_ids[:, None] == key_tiles[None, :]).astype(jnp.bfloat16)
            allowed = (
                jnp.einsum(
                    "hqj,jk->hqk", listed_rows, key_onehot, preferred_element_type=jnp.float32
                )
                > 0.5
            )
            result = attend_block(
                state_in, key_block, value_block, allowed, query_local, score_scale
            )
            return result

        return lax.fori_loop(0, block_count, one_block, state_now)

    return fold_step


def start_state(heads_here, block_len):
    top_all = jnp.full((heads_here, block_len), NEG_FLOOR, jnp.float32)
    total_all = jnp.zeros((heads_here, block_len), jnp.float32)
    accum_all = jnp.zeros((block_len, heads_here, HEAD_DIM), jnp.float32)
    return (top_all, total_all, accum_all)


def normalize(state_end):
    top_all, total_all, accum_all = state_end
    return (accum_all / jnp.transpose(total_all)[:, :, None]).astype(jnp.bfloat16)


def per_device(queries, keys, values, block_lists):
    row_count, col_count = queries.shape
    n_head = lax.axis_size("head")
    n_sub = lax.axis_size("sub")
    blk_index = lax.axis_index("blk")
    head_index = lax.axis_index("head")
    sub_index = lax.axis_index("sub")
    tile_total = block_lists.shape[1]
    heads_here = HEADS // (n_head * n_sub)
    block_len = row_count * n_head * n_sub

    def inward(tensor):
        return tensor.reshape(1, 1, row_count, n_head, n_sub, heads_here * HEAD_DIM)

    query_six, keys_six, values_six = (
        lax.all_to_all(
            lax.all_to_all(inward(queries), "head", split_axis=3, concat_axis=1, tiled=True),
            "sub",
            split_axis=4,
            concat_axis=0,
            tiled=True,
        ),
        lax.all_to_all(
            lax.all_to_all(inward(keys), "head", split_axis=3, concat_axis=1, tiled=True),
            "sub",
            split_axis=4,
            concat_axis=0,
            tiled=True,
        ),
        lax.all_to_all(
            lax.all_to_all(inward(values), "head", split_axis=3, concat_axis=1, tiled=True),
            "sub",
            split_axis=4,
            concat_axis=0,
            tiled=True,
        ),
    )
    query_local = query_six.reshape(block_len, heads_here, HEAD_DIM)
    keys_local = keys_six.reshape(block_len, heads_here, HEAD_DIM)
    values_local = values_six.reshape(block_len, heads_here, HEAD_DIM)

    def key_token(positions):
        source_dev = positions // block_len
        within = positions % block_len
        sub_source = within // (n_head * row_count)
        head_source = within // row_count % n_head
        offset = within % row_count
        return ((source_dev * n_head + head_source) * n_sub + sub_source) * row_count + offset

    query_tokens = key_token(blk_index * block_len + jnp.arange(block_len, dtype=jnp.int32))
    first_head = (head_index * n_sub + sub_index) * heads_here
    listed_rows = query_rows(block_lists, first_head, heads_here, query_tokens)
    fold_step = make_step(query_local, listed_rows, key_token, block_len, tile_total)
    state_end = fold_step(
        start_state(heads_here, block_len),
        (
            lax.all_gather(keys_local, "blk", axis=0, tiled=True),
            lax.all_gather(values_local, "blk", axis=0, tiled=True),
        ),
        jnp.int32(0),
    )
    result_rows = normalize(state_end)
    attended = result_rows.reshape(n_sub, n_head, row_count, 1, 1, heads_here * HEAD_DIM)
    returned = lax.all_to_all(
        lax.all_to_all(attended, "head", split_axis=1, concat_axis=3, tiled=True),
        "sub",
        split_axis=0,
        concat_axis=4,
        tiled=True,
    )
    return returned.reshape(row_count, col_count)


EXACT_COUNTS = tuple(range(12, 21))


def rank_of(rank, n_head, n_sub):
    line_count = n_head * n_sub
    return {
        "blk": rank // line_count,
        "head": rank // n_sub % n_head,
        "sub": rank % n_sub,
    }


def remote_copy(sizes, src, dst, send, recv, rank):
    return pltpu.make_async_remote_copy(
        src_ref=src,
        dst_ref=dst,
        send_sem=send,
        recv_sem=recv,
        device_id=rank_of(rank, sizes[1], sizes[2]),
        device_id_type=pl.DeviceIdType.MESH,
    )


def greet(sizes, rank):
    pl.semaphore_signal(
        pltpu.get_barrier_semaphore(), inc=1,
        device_id=rank_of(rank, sizes[1], sizes[2]),
        device_id_type=pl.DeviceIdType.MESH,
    )


def attend_tile(ids, query, buf):
    score_scale = 1.0 / math.sqrt(HEAD_DIM)
    scores, top = [], None
    for tile in ids:
        s = lax.dot_general(
            query, buf[1, tile], (((1,), (1,)), ((), ())), preferred_element_type=jnp.float32
        ) * score_scale
        scores.append(s)
        top = s if top is None else jnp.maximum(top, s)
    row_top = jnp.max(top, axis=1, keepdims=True)
    total, accum = None, None
    for e, tile in enumerate(ids):
        w = jnp.exp(scores[e] - row_top)
        if e:
            repeat = tile == ids[0]
            for f in range(1, e):
                repeat = jnp.logical_or(repeat, tile == ids[f])
            w = w * jnp.where(repeat, 0.0, 1.0)
        part = jnp.dot(
            w.astype(jnp.bfloat16), buf[2, tile], preferred_element_type=jnp.float32
        )
        total = w if total is None else total + w
        accum = part if accum is None else accum + part
    row_total = jnp.sum(total, axis=1, keepdims=True)
    return (accum / row_total).astype(jnp.bfloat16)


def general_kernel(sizes, entries, stage, list_rows, landed, lists, list_sem, *scratch):
    n_blk, n_head, n_sub = sizes
    line_count = n_head * n_sub
    count = n_blk * line_count
    heads_here = HEADS // count
    far_in = scratch[:heads_here]
    far_out = scratch[heads_here : 2 * heads_here]
    send_sem, recv_sem, local_sem = scratch[2 * heads_here :]
    line = lax.axis_index("head") * n_sub + lax.axis_index("sub")
    me = lax.axis_index("blk") * line_count + line

    def peer(d):
        return (me + d) % count

    def inward(t, a, target, sender):
        return remote_copy(
            sizes, stage.at[t, a * count + target], far_in[a].at[t, sender],
            send_sem.at[t, a, target], recv_sem.at[t, a, sender], target,
        )

    def outward(a, target, sender):
        return remote_copy(
            sizes, far_out[a].at[target], landed.at[a * count + sender],
            send_sem.at[3, a, target], recv_sem.at[3, a, sender], target,
        )

    def own_in(t, a):
        return pltpu.make_async_copy(
            stage.at[t, a * count + me], far_in[a].at[t, me], local_sem.at[t, a]
        )

    def own_out(a):
        return pltpu.make_async_copy(
            far_out[a].at[me], landed.at[a * count + me], local_sem.at[3, a]
        )

    def own_list(a):
        return pltpu.make_async_copy(
            list_rows.at[a * count + me], lists.at[a], list_sem.at[a]
        )

    def greet_all(d, carry):
        greet(sizes, peer(d))
        return carry

    lax.fori_loop(1, count, greet_all, 0)
    for a in range(heads_here):
        own_list(a).start()
    pl.semaphore_wait(pltpu.get_barrier_semaphore(), count - 1)

    for a in range(heads_here):
        def send_in(d, carry, a=a):
            for t in range(3):
                inward(t, a, peer(d), me).start()
            return carry

        lax.fori_loop(1, count, send_in, 0)
        for t in range(3):
            own_in(t, a).start()

    for a in range(heads_here):
        for t in range(3):
            own_in(t, a).wait()

        def arrive(d, carry, a=a):
            for t in range(3):
                inward(t, a, me, peer(d)).wait_recv()
            return carry

        lax.fori_loop(1, count, arrive, 0)
        own_list(a).wait()

        def one(i, a=a):
            ids = [lists[a, i * entries + e] for e in range(entries)]
            far_out[a][i] = attend_tile(ids, far_in[a][0, i], far_in[a])

        def work(d, carry, a=a, one=one):
            one(peer(d))

            @pl.when(d > 1)
            def _():
                outward(a, peer(d - 1), me).start()

            return carry

        lax.fori_loop(1, count, work, 0)
        one(me)
        outward(a, peer(count - 1), me).start()
        own_out(a).start()

    for a in range(heads_here):
        own_out(a).wait()

        def finish(d, carry, a=a):
            for t in range(3):
                inward(t, a, peer(d), me).wait_send()
            outward(a, peer(d), me).wait_send()
            outward(a, me, peer(d)).wait_recv()
            return carry

        lax.fori_loop(1, count, finish, 0)


def general_exchange(sizes, collective_id, queries, keys, values, block_lists, table):
    count = sizes[0] * sizes[1] * sizes[2]
    rows = queries.shape[0]
    block = (rows, HEAD_DIM)
    heads_here = HEADS // count
    stage = jnp.stack(
        [jnp.swapaxes(x.reshape(rows, HEADS, HEAD_DIM), 0, 1) for x in (queries, keys, values)]
    )
    list_rows = block_lists.reshape(HEADS, -1)
    anywhere = pl.BlockSpec(memory_space=pl.ANY)
    dma = pltpu.SemaphoreType.DMA
    scratch = [pltpu.SMEM((heads_here, list_rows.shape[1]), jnp.int32), dma((heads_here,))]
    scratch += [pltpu.VMEM((3, count) + block, jnp.bfloat16)] * heads_here
    scratch += [pltpu.VMEM((count,) + block, jnp.bfloat16)] * heads_here
    scratch += [dma((4, heads_here, count))] * 2 + [dma((4, heads_here))]
    landed = pl.pallas_call(
        functools.partial(general_kernel, sizes, block_lists.shape[2]),
        out_shape=jax.ShapeDtypeStruct((HEADS,) + block, jnp.bfloat16),
        in_specs=[anywhere, anywhere],
        out_specs=anywhere,
        scratch_shapes=scratch,
        compiler_params=pltpu.CompilerParams(
            collective_id=collective_id, has_side_effects=True
        ),
    )(stage, list_rows)
    return jnp.swapaxes(landed, 0, 1).reshape(rows, HEADS * HEAD_DIM)


def split_kernel(sizes, near, q_hbm, k_hbm, v_hbm, table_ref, out_ref, table, stage, q_all, k_all,
                 v_all, near_query, near_kv, near_out, far_in, far_out, landed, local_sem,
                 near_send, near_recv, near_back_send, near_back_recv, hop_send, hop_recv,
                 far_send, far_recv, far_back_send, far_back_recv):
    n_blk, n_head, n_sub = sizes
    line_count = n_head * n_sub
    far = HEADS - near
    near_slots = -(-near // line_count)
    far_slots = -(-far // n_blk)
    score_scale = 1.0 / math.sqrt(HEAD_DIM)

    blk, sub = lax.axis_index("blk"), lax.axis_index("sub")
    line = lax.axis_index("head") * n_sub + sub
    first = blk * line_count
    me = first + line

    def near_number(a, target_line):
        return a * line_count + target_line % n_sub * n_head + target_line // n_sub

    def far_number(a, target_blk):
        mirrored = target_blk + sub % 2 * (n_blk - 1 - 2 * target_blk)
        return a * n_blk + (mirrored + n_blk - 1) % n_blk

    def line_peer(d):
        return (line + d) % line_count

    def blk_peer(d):
        return (blk + d) % n_blk

    def if_near(a, target_line, action):
        pl.when(near_number(a, target_line) < near)(action)

    def if_far(a, target_blk, action):
        pl.when(far_number(a, target_blk) < far)(action)

    def near_inward(t, a, target, sender):
        number = near_number(a, target)
        if t:
            source, slot = stage.at[number, pl.ds(0, 2)], near_kv.at[a, 1, sender]
        else:
            source, slot = stage.at[number, 2], near_query.at[a, sender]
        return remote_copy(
            sizes, source, slot, near_send.at[t, a, target], near_recv.at[t, a, sender],
            first + target,
        )

    def near_outward(a, target, sender):
        return remote_copy(
            sizes, near_out.at[a, target], landed.at[near_number(a, sender)],
            near_back_send.at[a, target], near_back_recv.at[a, sender], first + target,
        )

    def hop(a, direction):
        step = 1 - 2 * direction
        return remote_copy(
            sizes, near_kv.at[a, 1], near_kv.at[a, 1 - step],
            hop_send.at[a, direction], hop_recv.at[a, direction],
            (blk + n_blk + step) % n_blk * line_count + line,
        )

    def each_hop(action, sending):
        up, down = blk < n_blk - 1, blk > 0
        pl.when(up if sending else down)(functools.partial(action, 0))
        pl.when(down if sending else up)(functools.partial(action, 1))

    def far_inward(a, target, sender):
        return remote_copy(
            sizes, stage.at[near + far_number(a, target)], far_in.at[a, sender],
            far_send.at[a, target], far_recv.at[a, sender], target * line_count + line,
        )

    def far_outward(a, target, sender):
        return remote_copy(
            sizes, far_out.at[a, target], landed.at[near + far_number(a, sender)],
            far_back_send.at[a, target], far_back_recv.at[a, sender],
            target * line_count + line,
        )

    table_load = pltpu.make_async_copy(table_ref, table, local_sem.at[0])
    table_load.start()
    sources = ((k_hbm, k_all), (v_hbm, v_all), (q_hbm, q_all))

    def load_head(h, carry):
        where = pl.ds(pl.multiple_of(h * HEAD_DIM, HEAD_DIM), HEAD_DIM)
        for t, (source, held) in enumerate(sources):
            pltpu.make_async_copy(source.at[:, where], held.at[h], local_sem.at[1 + t]).start()
        return carry

    lax.fori_loop(0, HEADS, load_head, 0)
    for d in range(1, line_count):
        greet(sizes, first + line_peer(d))
    for d in range(1, n_blk):
        greet(sizes, blk_peer(d) * line_count + line)

    def clear(edge):
        def clear_tile(i, carry):
            near_kv[i // line_count, edge, i % line_count] = jnp.zeros(
                near_kv.shape[3:], near_kv.dtype
            )
            return carry

        lax.fori_loop(0, near_slots * line_count, clear_tile, 0)

    pl.when(blk == 0)(functools.partial(clear, 0))
    pl.when(blk == n_blk - 1)(functools.partial(clear, 2))
    table_load.wait()
    for t, (source, held) in enumerate(sources):
        pltpu.make_async_copy(landed, held, local_sem.at[1 + t]).wait()
    pl.semaphore_wait(pltpu.get_barrier_semaphore(), line_count + n_blk - 2)

    def put_stage(slot):
        head = table[0, slot]
        for t, source in enumerate((k_all, v_all, q_all)):
            stage[slot, t] = source[head]

    def each_other(count, peer, test, action):
        def one(d, carry):
            test(peer(d), lambda: action(peer(d)))
            return carry

        lax.fori_loop(1, count, one, 0)

    def other_far(a, action):
        each_other(n_blk, blk_peer, functools.partial(if_far, a), action)

    def other_near(a, action):
        each_other(line_count, line_peer, functools.partial(if_near, a), action)

    def stage_far(a):
        def own():
            head = table[0, near + far_number(a, blk)]
            for t, source in enumerate((k_all, v_all, q_all)):
                far_in[a, blk, t] = source[head]

        other_far(a, lambda target: put_stage(near + far_number(a, target)))
        if_far(a, blk, own)

    def stage_near(a):
        def own():
            head = table[0, near_number(a, line)]
            near_kv[a, 1, line, 0] = k_all[head]
            near_kv[a, 1, line, 1] = v_all[head]
            near_query[a, line] = q_all[head]

        other_near(a, lambda target: put_stage(near_number(a, target)))
        if_near(a, line, own)

    def send_far(a):
        other_far(a, lambda target: far_inward(a, target, blk).start())

    def send_near(a):
        for t in (1, 0):
            other_near(a, lambda target, t=t: near_inward(t, a, target, line).start())

    def fill(a, carry):
        pl.when(a < far_slots)(lambda: stage_far(a))
        pl.when(jnp.logical_and(a > 0, a <= near_slots))(lambda: send_near(a - 1))
        pl.when(a < near_slots)(lambda: stage_near(a))
        pl.when(a < far_slots)(lambda: send_far(a))
        return carry

    lax.fori_loop(0, max(near_slots + 1, far_slots), fill, 0)

    def finish_tile(scores, values):
        top = None
        for s in scores:
            top = s if top is None else jnp.maximum(top, s)
        row_top = jnp.max(top, axis=1, keepdims=True)
        total, accum = None, None
        for s, value in zip(scores, values):
            w = jnp.exp(s - row_top)
            part = jnp.dot(
                w.astype(jnp.bfloat16), value(), preferred_element_type=jnp.float32
            )
            total = w if total is None else total + w
            accum = part if accum is None else accum + part
        row_total = jnp.sum(total, axis=1, keepdims=True)
        return (accum / row_total).astype(jnp.bfloat16)

    def score(query, key, bits, place):
        s = lax.dot_general(
            query, key, (((1,), (1,)), ((), ())), preferred_element_type=jnp.float32
        )
        return s * score_scale + jnp.where((bits >> place) % 2 == 1, 0.0, NEG_FLOOR)

    def far_tile(a, source):
        bits = table[8 + source * line_count + line, near + far_number(a, blk)]
        query = far_in[a, source, 2]
        scores = [
            score(query, far_in[a, c, 0], bits, c * line_count + line) for c in range(n_blk)
        ]
        return finish_tile(
            scores, [lambda c=c: far_in[a, c, 1] for c in range(n_blk)]
        )

    def near_tile(a, source):
        bits = table[8 + first + source, near_number(a, line)] * (1 << line_count)
        query = near_query[a, source]
        pairs = [(f, c) for f in (1, 0, 2) for c in range(line_count)]
        scores = [
            score(query, near_kv[a, f, c, 0], bits, first + f * line_count + c) for f, c in pairs
        ]
        return finish_tile(scores, [lambda f=f, c=c: near_kv[a, f, c, 1] for f, c in pairs])

    def near_whole(a):
        def whole():
            def arrive(d, carry):
                near_inward(1, a, line, line_peer(d)).wait_recv()
                return carry

            lax.fori_loop(1, line_count, arrive, 0)
            each_hop(lambda direction: hop(a, direction).start(), True)

        pl.when(a < near_slots)(lambda: if_near(a, line, whole))

    def far_work(a):
        def whole():
            number = far_number(a, blk)

            def arrive(d, carry):
                far_inward(a, blk, blk_peer(d)).wait_recv()
                return carry

            lax.fori_loop(1, n_blk, arrive, 0)

            def work(d, carry):
                result = far_tile(a, blk_peer(d))

                @pl.when(d < n_blk)
                def _():
                    far_out[a, blk_peer(d)] = result

                @pl.when(d == n_blk)
                def _():
                    landed[near + number] = result

                @pl.when(d > 1)
                def _():
                    far_outward(a, blk_peer(d - 1), blk).start()

                return carry

            lax.fori_loop(1, n_blk + 1, work, 0)

        pl.when(a < far_slots)(lambda: if_far(a, blk, whole))

    def first_half(a, carry):
        near_whole(2 * a)
        near_whole(2 * a + 1)
        far_work(a)
        return carry

    lax.fori_loop(0, max(far_slots, -(-near_slots // 2)), first_half, 0)

    def second_half(a, carry):
        def whole():
            number = near_number(a, line)
            each_hop(lambda direction: hop(a, direction).wait_recv(), False)

            def arrive(d, carry):
                near_inward(0, a, line, line_peer(d)).wait_recv()
                return carry

            lax.fori_loop(1, line_count, arrive, 0)

            def work(d, carry):
                result = near_tile(a, line_peer(d))

                @pl.when(d < line_count)
                def _():
                    near_out[a, line_peer(d)] = result

                @pl.when(d == line_count)
                def _():
                    landed[number] = result

                @pl.when(d > 1)
                def _():
                    near_outward(a, line_peer(d - 1), line).start()

                return carry

            lax.fori_loop(1, line_count + 1, work, 0)

        if_near(a, line, whole)
        return carry

    lax.fori_loop(0, near_slots, second_half, 0)

    def finish_far(a, carry):
        def own():
            def sent(d, carry):
                far_outward(a, blk_peer(d), blk).wait_send()
                return carry

            lax.fori_loop(1, n_blk, sent, 0)

        def other(target):
            far_inward(a, target, blk).wait_send()
            far_outward(a, blk, target).wait_recv()

        if_far(a, blk, own)
        other_far(a, other)
        return carry

    def finish_near(a, carry):
        def own():
            def sent(d, carry):
                near_outward(a, line_peer(d), line).wait_send()
                return carry

            lax.fori_loop(1, line_count, sent, 0)
            each_hop(lambda direction: hop(a, direction).wait_send(), True)

        def other(target):
            near_inward(1, a, target, line).wait_send()
            near_inward(0, a, target, line).wait_send()
            near_outward(a, line, target).wait_recv()

        if_near(a, line, own)
        other_near(a, other)
        return carry

    lax.fori_loop(0, near_slots, finish_near, 0)
    lax.fori_loop(0, far_slots, finish_far, 0)

    def restore(i, carry):
        for e in range(4):
            h = i * 4 + e
            where = pl.ds(pl.multiple_of(h * HEAD_DIM, HEAD_DIM), HEAD_DIM)
            out_ref[:, where] = landed[table[1, h]]
        return carry

    lax.fori_loop(0, HEADS // 4, restore, 0)


def split_exchange(sizes, near, collective_id, queries, keys, values, block_lists, table):
    n_blk, line_count = sizes[0], sizes[1] * sizes[2]
    rows, width = queries.shape
    near_slots = -(-near // line_count)
    far_slots = -(-(HEADS - near) // n_blk)
    block = (rows, HEAD_DIM)
    anywhere = pl.BlockSpec(memory_space=pl.ANY)
    dma = pltpu.SemaphoreType.DMA

    def buffer(*lead):
        return pltpu.VMEM(lead + block, jnp.bfloat16)

    return pl.pallas_call(
        functools.partial(split_kernel, sizes, near),
        out_shape=jax.ShapeDtypeStruct((rows, width), jnp.bfloat16),
        in_specs=[anywhere] * 4,
        out_specs=pl.BlockSpec(memory_space=pltpu.VMEM),
        scratch_shapes=[
            pltpu.SMEM(table.shape, jnp.int32),
            buffer(HEADS, 3),
            buffer(HEADS),
            buffer(HEADS),
            buffer(HEADS),
            buffer(near_slots, line_count),
            buffer(near_slots, 3, line_count, 2),
            buffer(near_slots, line_count),
            buffer(far_slots, n_blk, 3),
            buffer(far_slots, n_blk),
            buffer(HEADS),
            dma((4,)),
            dma((2, near_slots, line_count)),
            dma((2, near_slots, line_count)),
            dma((near_slots, line_count)),
            dma((near_slots, line_count)),
            dma((near_slots, 2)),
            dma((near_slots, 2)),
            dma((far_slots, n_blk)),
            dma((far_slots, n_blk)),
            dma((far_slots, n_blk)),
            dma((far_slots, n_blk)),
        ],
        compiler_params=pltpu.CompilerParams(
            collective_id=collective_id, has_side_effects=True
        ),
    )(queries, keys, values, table)


def sort_kernel(frames, line_count, entries, lists_ref, table, choice):
    ids = lists_ref[...]
    steps, heads = ids.shape
    tiles = steps // entries
    per_frame = steps // frames
    away = None
    for f in range(frames):
        part = ids[f * per_frame : (f + 1) * per_frame]
        outside = jnp.logical_or(part < (f - 1) * line_count, part >= (f + 2) * line_count)
        found = jnp.max(jnp.where(outside, 1, 0), axis=0, keepdims=True)
        away = found if away is None else jnp.maximum(away, found)
    row = lax.broadcasted_iota(jnp.int32, (heads, heads), 0)
    col = lax.broadcasted_iota(jnp.int32, (heads, heads), 1)
    away_col = jnp.broadcast_to(away, (heads, heads))
    away_row = jnp.broadcast_to(
        jnp.sum(jnp.where(row == col, away_col, 0), axis=1, keepdims=True), (heads, heads)
    )
    same = away_row == away_col
    ahead = jnp.where(same, jnp.where(row < col, 1, 0), away_col)
    place = jnp.sum(ahead, axis=0, keepdims=True)
    behind = jnp.where(same, jnp.where(col < row, 1, 0), away_row)
    place_of_row = jnp.sum(behind, axis=1, keepdims=True)
    perm = jnp.sum(
        jnp.where(jnp.broadcast_to(place_of_row, (heads, heads)) == col, row, 0),
        axis=0, keepdims=True,
    )
    table[0:1, 0:heads] = perm
    table[1:2, 0:heads] = place
    bits = None
    for e in range(entries):
        bit = jnp.left_shift(1, lists_ref[pl.ds(e, tiles, stride=entries), :])
        bits = bit if bits is None else jnp.bitwise_or(bits, bit)
    picks = jnp.where(jnp.broadcast_to(place, (heads, heads)) == row, 1.0, 0.0).astype(jnp.bfloat16)
    low, high = [
        lax.dot_general(
            part.astype(jnp.float32).astype(jnp.bfloat16), picks, (((1,), (1,)), ((), ())),
            preferred_element_type=jnp.float32,
        ).astype(jnp.int32)
        for part in (jnp.bitwise_and(bits, 255), jnp.right_shift(bits, 8))
    ]
    table[8 : 8 + tiles, 0:heads] = low + high * 256
    near = heads - jnp.sum(away.astype(jnp.float32)).astype(jnp.int32)
    least, most = EXACT_COUNTS[0], EXACT_COUNTS[-1]
    known = jnp.logical_and(near >= least, near <= most)
    choice[0] = jnp.where(known, near - least, most - least + 1)


def sort_heads(line_count, block_lists):
    heads, tiles, entries = block_lists.shape
    by_row = jnp.transpose(block_lists, (1, 2, 0)).reshape(tiles * entries, heads)
    vmem = pl.BlockSpec(memory_space=pltpu.VMEM)
    return pl.pallas_call(
        functools.partial(sort_kernel, tiles // line_count, line_count, entries),
        out_shape=(
            jax.ShapeDtypeStruct((8 + tiles, 128), jnp.int32),
            jax.ShapeDtypeStruct((1,), jnp.int32),
        ),
        in_specs=[vmem],
        out_specs=(vmem, pl.BlockSpec(memory_space=pltpu.SMEM)),
    )(by_row)


def solution(mesh):
    sizes = tuple(mesh.shape[axis] for axis in ("blk", "head", "sub"))
    line_count = sizes[1] * sizes[2]
    count = sizes[0] * line_count

    def body(queries, keys, values, block_lists):
        fits = queries.shape[0] == TILE and HEADS % count == 0 and count <= 16
        if not fits or block_lists.shape[1] != count:
            return per_device(queries, keys, values, block_lists)
        table, choice = sort_heads(line_count, block_lists)
        branches = [
            functools.partial(split_exchange, sizes, n, number)
            for number, n in enumerate(EXACT_COUNTS)
        ]
        branches.append(functools.partial(general_exchange, sizes, len(EXACT_COUNTS)))
        return lax.switch(choice[0], branches, queries, keys, values, block_lists, table)

    spec = P(("grp", "blk", "head", "sub"), None)
    return jax.shard_map(
        body, mesh=mesh, in_specs=(spec, spec, spec, P()), out_specs=spec, check_vma=False
    )
```

```python
import functools
import math

import jax
import jax.numpy as jnp
from jax import lax
from jax.experimental import pallas as pl
from jax.experimental.pallas import tpu as pltpu
from jax.sharding import PartitionSpec as P

HEADS = 32
HEAD_DIM = 128
TILE = 128


NEG_FLOOR = -1e30


def query_rows(block_lists, first_head, heads_here, query_tokens):
    tile_ids = jnp.arange(block_lists.shape[1], dtype=jnp.int32)
    lists_local = lax.dynamic_slice_in_dim(block_lists, first_head, heads_here, 0)
    tile_mask = jnp.any(lists_local[:, :, :, None] == tile_ids, axis=2).astype(jnp.bfloat16)
    query_onehot = ((query_tokens // TILE)[:, None] == tile_ids[None, :]).astype(jnp.bfloat16)
    listed = jnp.einsum("qi,hij->hqj", query_onehot, tile_mask, preferred_element_type=jnp.float32)
    return listed.astype(jnp.bfloat16)


def attend_block(state_now, key_block, value_block, allowed, query_local, score_scale):
    top_old, total_old, accum_old = state_now
    scores = (
        jnp.einsum("qhd,khd->hqk", query_local, key_block, preferred_element_type=jnp.float32)
        * score_scale
    )
    top_new = jnp.maximum(top_old, jnp.max(jnp.where(allowed, scores, NEG_FLOOR), axis=2))
    factor = jnp.exp(top_old - top_new)
    weights = jnp.where(allowed, jnp.exp(scores - top_new[:, :, None]), 0.0)
    total_new = total_old * factor + jnp.sum(weights, axis=2)
    product = jnp.einsum(
        "hqk,khd->qhd",
        weights.astype(jnp.bfloat16),
        value_block,
        preferred_element_type=jnp.float32,
    )
    accum_new = accum_old * jnp.transpose(factor)[:, :, None] + product
    return (top_new, total_new, accum_new)


def make_step(query_local, listed_rows, key_token, block_len, tile_total):
    score_scale = 1.0 / math.sqrt(HEAD_DIM)
    tile_ids = jnp.arange(tile_total, dtype=jnp.int32)

    def fold_step(state_now, piece, first_row):
        key_piece, value_piece = piece
        block_count = key_piece.shape[0] // block_len

        def one_block(block_index, state_in):
            key_block = lax.dynamic_slice_in_dim(key_piece, block_index * block_len, block_len, 0)
            value_block = lax.dynamic_slice_in_dim(
                value_piece, block_index * block_len, block_len, 0
            )
            positions = block_index * block_len + jnp.arange(block_len, dtype=jnp.int32)
            key_tiles = key_token(positions) // TILE
            key_onehot = (tile_ids[:, None] == key_tiles[None, :]).astype(jnp.bfloat16)
            allowed = (
                jnp.einsum(
                    "hqj,jk->hqk", listed_rows, key_onehot, preferred_element_type=jnp.float32
                )
                > 0.5
            )
            result = attend_block(
                state_in, key_block, value_block, allowed, query_local, score_scale
            )
            return result

        return lax.fori_loop(0, block_count, one_block, state_now)

    return fold_step


def start_state(heads_here, block_len):
    top_all = jnp.full((heads_here, block_len), NEG_FLOOR, jnp.float32)
    total_all = jnp.zeros((heads_here, block_len), jnp.float32)
    accum_all = jnp.zeros((block_len, heads_here, HEAD_DIM), jnp.float32)
    return (top_all, total_all, accum_all)


def normalize(state_end):
    top_all, total_all, accum_all = state_end
    return (accum_all / jnp.transpose(total_all)[:, :, None]).astype(jnp.bfloat16)


def per_device(queries, keys, values, block_lists):
    row_count, col_count = queries.shape
    n_head = lax.axis_size("head")
    n_sub = lax.axis_size("sub")
    blk_index = lax.axis_index("blk")
    head_index = lax.axis_index("head")
    sub_index = lax.axis_index("sub")
    tile_total = block_lists.shape[1]
    heads_here = HEADS // (n_head * n_sub)
    block_len = row_count * n_head * n_sub

    def inward(tensor):
        return tensor.reshape(1, 1, row_count, n_head, n_sub, heads_here * HEAD_DIM)

    query_six, keys_six, values_six = (
        lax.all_to_all(
            lax.all_to_all(inward(queries), "head", split_axis=3, concat_axis=1, tiled=True),
            "sub",
            split_axis=4,
            concat_axis=0,
            tiled=True,
        ),
        lax.all_to_all(
            lax.all_to_all(inward(keys), "head", split_axis=3, concat_axis=1, tiled=True),
            "sub",
            split_axis=4,
            concat_axis=0,
            tiled=True,
        ),
        lax.all_to_all(
            lax.all_to_all(inward(values), "head", split_axis=3, concat_axis=1, tiled=True),
            "sub",
            split_axis=4,
            concat_axis=0,
            tiled=True,
        ),
    )
    query_local = query_six.reshape(block_len, heads_here, HEAD_DIM)
    keys_local = keys_six.reshape(block_len, heads_here, HEAD_DIM)
    values_local = values_six.reshape(block_len, heads_here, HEAD_DIM)

    def key_token(positions):
        source_dev = positions // block_len
        within = positions % block_len
        sub_source = within // (n_head * row_count)
        head_source = within // row_count % n_head
        offset = within % row_count
        return ((source_dev * n_head + head_source) * n_sub + sub_source) * row_count + offset

    query_tokens = key_token(blk_index * block_len + jnp.arange(block_len, dtype=jnp.int32))
    first_head = (head_index * n_sub + sub_index) * heads_here
    listed_rows = query_rows(block_lists, first_head, heads_here, query_tokens)
    fold_step = make_step(query_local, listed_rows, key_token, block_len, tile_total)
    state_end = fold_step(
        start_state(heads_here, block_len),
        (
            lax.all_gather(keys_local, "blk", axis=0, tiled=True),
            lax.all_gather(values_local, "blk", axis=0, tiled=True),
        ),
        jnp.int32(0),
    )
    result_rows = normalize(state_end)
    attended = result_rows.reshape(n_sub, n_head, row_count, 1, 1, heads_here * HEAD_DIM)
    returned = lax.all_to_all(
        lax.all_to_all(attended, "head", split_axis=1, concat_axis=3, tiled=True),
        "sub",
        split_axis=0,
        concat_axis=4,
        tiled=True,
    )
    return returned.reshape(row_count, col_count)


EXACT_COUNTS = tuple(range(10, 23))


def rank_of(rank, n_head, n_sub):
    line_count = n_head * n_sub
    return {
        "blk": rank // line_count,
        "head": rank // n_sub % n_head,
        "sub": rank % n_sub,
    }


def remote_copy(sizes, src, dst, send, recv, rank):
    return pltpu.make_async_remote_copy(
        src_ref=src,
        dst_ref=dst,
        send_sem=send,
        recv_sem=recv,
        device_id=rank_of(rank, sizes[1], sizes[2]),
        device_id_type=pl.DeviceIdType.MESH,
    )


def greet(sizes, rank):
    pl.semaphore_signal(
        pltpu.get_barrier_semaphore(), inc=1,
        device_id=rank_of(rank, sizes[1], sizes[2]),
        device_id_type=pl.DeviceIdType.MESH,
    )


def attend_tile(ids, query, buf):
    score_scale = 1.0 / math.sqrt(HEAD_DIM)
    scores, top = [], None
    for tile in ids:
        s = lax.dot_general(
            query, buf[0, tile], (((1,), (1,)), ((), ())), preferred_element_type=jnp.float32
        ) * score_scale
        scores.append(s)
        top = s if top is None else jnp.maximum(top, s)
    row_top = jnp.max(top, axis=1, keepdims=True)
    total, accum = None, None
    for e, tile in enumerate(ids):
        w = jnp.exp(scores[e] - row_top)
        if e:
            repeat = tile == ids[0]
            for f in range(1, e):
                repeat = jnp.logical_or(repeat, tile == ids[f])
            w = w * jnp.where(repeat, 0.0, 1.0)
        part = jnp.dot(
            w.astype(jnp.bfloat16), buf[1, tile], preferred_element_type=jnp.float32
        )
        total = w if total is None else total + w
        accum = part if accum is None else accum + part
    row_total = jnp.sum(total, axis=1, keepdims=True)
    return (accum / row_total).astype(jnp.bfloat16)


def general_kernel(sizes, entries, stage, list_rows, landed, lists, list_sem, *scratch):
    n_blk, n_head, n_sub = sizes
    line_count = n_head * n_sub
    count = n_blk * line_count
    heads_here = HEADS // count
    far_in = scratch[:heads_here]
    far_out = scratch[heads_here : 2 * heads_here]
    send_sem, recv_sem, local_sem = scratch[2 * heads_here :]
    line = lax.axis_index("head") * n_sub + lax.axis_index("sub")
    me = lax.axis_index("blk") * line_count + line

    def peer(d):
        return (me + d) % count

    def inward(t, a, target, sender):
        return remote_copy(
            sizes, stage.at[t, a * count + target], far_in[a].at[t, sender],
            send_sem.at[t, a, target], recv_sem.at[t, a, sender], target,
        )

    def outward(a, target, sender):
        return remote_copy(
            sizes, far_out[a].at[target], landed.at[a * count + sender],
            send_sem.at[3, a, target], recv_sem.at[3, a, sender], target,
        )

    def own_in(t, a):
        return pltpu.make_async_copy(
            stage.at[t, a * count + me], far_in[a].at[t, me], local_sem.at[t, a]
        )

    def own_out(a):
        return pltpu.make_async_copy(
            far_out[a].at[me], landed.at[a * count + me], local_sem.at[3, a]
        )

    def own_list(a):
        return pltpu.make_async_copy(
            list_rows.at[a * count + me], lists.at[a], list_sem.at[a]
        )

    def greet_all(d, carry):
        greet(sizes, peer(d))
        return carry

    lax.fori_loop(1, count, greet_all, 0)
    for a in range(heads_here):
        own_list(a).start()
    pl.semaphore_wait(pltpu.get_barrier_semaphore(), count - 1)

    for a in range(heads_here):
        def send_in(d, carry, a=a):
            for t in range(3):
                inward(t, a, peer(d), me).start()
            return carry

        lax.fori_loop(1, count, send_in, 0)
        for t in range(3):
            own_in(t, a).start()

    for a in range(heads_here):
        for t in range(3):
            own_in(t, a).wait()

        def arrive(d, carry, a=a):
            for t in range(3):
                inward(t, a, me, peer(d)).wait_recv()
            return carry

        lax.fori_loop(1, count, arrive, 0)
        own_list(a).wait()

        def one(i, a=a):
            ids = [lists[a, i * entries + e] for e in range(entries)]
            far_out[a][i] = attend_tile(ids, far_in[a][2, i], far_in[a])

        def work(d, carry, a=a, one=one):
            one(peer(d))

            @pl.when(d > 1)
            def _():
                outward(a, peer(d - 1), me).start()

            return carry

        lax.fori_loop(1, count + 1, work, 0)
        own_out(a).start()

    for a in range(heads_here):
        own_out(a).wait()

        def finish(d, carry, a=a):
            for t in range(3):
                inward(t, a, peer(d), me).wait_send()
            outward(a, peer(d), me).wait_send()
            outward(a, me, peer(d)).wait_recv()
            return carry

        lax.fori_loop(1, count, finish, 0)


def general_exchange(sizes, collective_id, block_lists, table, keys, values, queries):
    count = sizes[0] * sizes[1] * sizes[2]
    rows = keys.shape[0]
    stage = jnp.stack([keys, values, queries]).reshape(3, rows, HEADS, HEAD_DIM)
    stage = jnp.swapaxes(stage, 1, 2)
    block = (rows, HEAD_DIM)
    heads_here = HEADS // count
    list_rows = block_lists.reshape(HEADS, -1)
    anywhere = pl.BlockSpec(memory_space=pl.ANY)
    dma = pltpu.SemaphoreType.DMA
    scratch = [pltpu.SMEM((heads_here, list_rows.shape[1]), jnp.int32), dma((heads_here,))]
    scratch += [pltpu.VMEM((3, count) + block, jnp.bfloat16)] * heads_here
    scratch += [pltpu.VMEM((count,) + block, jnp.bfloat16)] * heads_here
    scratch += [dma((4, heads_here, count))] * 2 + [dma((4, heads_here))]
    landed = pl.pallas_call(
        functools.partial(general_kernel, sizes, block_lists.shape[2]),
        out_shape=jax.ShapeDtypeStruct((HEADS,) + block, jnp.bfloat16),
        in_specs=[anywhere, anywhere],
        out_specs=anywhere,
        scratch_shapes=scratch,
        compiler_params=pltpu.CompilerParams(
            collective_id=collective_id, has_side_effects=True
        ),
    )(stage, list_rows)
    return jnp.swapaxes(landed, 0, 1).reshape(rows, HEADS * HEAD_DIM)


def split_kernel(sizes, near, table_ref, k_all, v_hbm, q_hbm, out_ref, table, v_all, q_all, by_head, stage, near_in, near_side,
                 near_out, far_in, far_out, landed, local_sem, below_sem, above_sem, near_send, near_recv, near_back,
                 hop_send, hop_recv, far_send, far_recv, far_back):
    n_blk, n_head, n_sub = sizes
    line_count = n_head * n_sub
    far = HEADS - near
    near_slots = -(-near // line_count)
    far_slots = -(-far // n_blk)
    score_scale = 1.0 / math.sqrt(HEAD_DIM)

    blk, sub = lax.axis_index("blk"), lax.axis_index("sub")
    line = lax.axis_index("head") * n_sub + sub
    first = blk * line_count

    def near_number(a, target_line):
        return a * line_count + target_line % n_sub * n_head + target_line // n_sub

    def far_number(a, target_blk):
        mirrored = target_blk + sub % 2 * (n_blk - 1 - 2 * target_blk)
        return a * n_blk + (mirrored + n_blk - 1) % n_blk

    def line_peer(d):
        return (line + d) % line_count

    def blk_peer(d):
        return (blk + d) % n_blk

    def if_near(a, target_line, action):
        pl.when(near_number(a, target_line) < near)(action)

    def if_far(a, target_blk, action):
        pl.when(far_number(a, target_blk) < far)(action)

    def each_other(count, peer, test, action):
        def one(d, carry):
            test(peer(d), lambda: action(peer(d)))
            return carry

        lax.fori_loop(1, count, one, 0)

    def other_far(a, action):
        each_other(n_blk, blk_peer, functools.partial(if_far, a), action)

    def other_near(a, action):
        each_other(line_count, line_peer, functools.partial(if_near, a), action)

    def take(sem, unit, pieces):
        if pieces:
            part = unit.at[pl.ds(0, pieces)]
            pltpu.make_async_copy(part, part, sem).wait()

    def take_others(sem, unit, a, own, total, count):
        rest = total % count
        if total >= count:
            pl.when(a < total // count)(lambda: take(sem, unit, count - 1))
        if rest:
            last = a == total // count
            pl.when(jnp.logical_and(last, own < total))(lambda: take(sem, unit, rest - 1))
            pl.when(jnp.logical_and(last, own >= total))(lambda: take(sem, unit, rest))

    def take_far(sem, unit, a):
        take_others(sem, unit, a, far_number(a, blk), far, n_blk)

    def take_near(sem, unit, a):
        take_others(sem, unit, a, near_number(a, line), near, line_count)

    def near_inward(a, t, target):
        return remote_copy(
            sizes, stage.at[near_number(a, target), t], near_in.at[a, line, t],
            near_send.at[a], near_recv.at[a], first + target,
        )

    def near_outward(a, target):
        return remote_copy(
            sizes, near_out.at[a, target], landed.at[near_number(a, line)],
            near_send.at[a], near_back.at[a], first + target,
        )

    def hop(a, direction):
        step = 1 - 2 * direction
        return remote_copy(
            sizes, near_in.at[a, :, pl.ds(0, 2)], near_side.at[a, direction],
            hop_send.at[a, direction], hop_recv.at[a, direction],
            (blk + n_blk + step) % n_blk * line_count + line,
        )

    def each_hop(action, sending):
        up, down = blk < n_blk - 1, blk > 0
        pl.when(up if sending else down)(functools.partial(action, 0))
        pl.when(down if sending else up)(functools.partial(action, 1))

    def far_inward(a, t, target):
        return remote_copy(
            sizes, stage.at[near + far_number(a, target), t], far_in.at[a, blk, t],
            far_send.at[a], far_recv.at[a], target * line_count + line,
        )

    def far_outward(a, target):
        return remote_copy(
            sizes, far_out.at[a, target], landed.at[near + far_number(a, blk)],
            far_send.at[a], far_back.at[a], target * line_count + line,
        )

    last = n_blk - 1
    below, above = (blk > 0).astype(jnp.int32), (blk < last).astype(jnp.int32)
    pl.when(blk < last)(lambda: greet(sizes, first + line_count + line))
    pl.when(blk > 0)(lambda: greet(sizes, first - line_count + line))
    for d in range(1, line_count):
        greet(sizes, first + line_peer(d))
    loads = [
        pltpu.make_async_copy(table_ref, table, local_sem.at[0]),
        pltpu.make_async_copy(v_hbm, v_all, local_sem.at[1]),
        pltpu.make_async_copy(q_hbm, q_all, local_sem.at[2]),
    ]
    for load in loads:
        load.start()

    def clear(side):
        def clear_tile(i, carry):
            near_side[i // line_count, side, i % line_count] = jnp.zeros(
                near_side.shape[3:], near_side.dtype
            )
            return carry

        lax.fori_loop(0, near_slots * line_count, clear_tile, 0)

    def columns(h):
        return pl.ds(pl.multiple_of(h * HEAD_DIM, HEAD_DIM), HEAD_DIM)

    def split_heads(t, source):
        def split_head(h, carry):
            by_head[t, h] = source[:, columns(h)]
            return carry

        lax.fori_loop(0, HEADS, split_head, 0)

    def pass_on(step, sem):
        def tell():
            pl.semaphore_signal(
                sem, inc=1,
                device_id=rank_of(first + step * line_count + line, n_head, n_sub),
                device_id_type=pl.DeviceIdType.MESH,
            )

        def heard(e, carry):
            pl.semaphore_wait(sem, 1)
            pl.when(blk < last if step > 0 else blk > 0)(tell)
            return carry

        known = blk if step > 0 else last - blk
        pl.when(jnp.logical_and(blk > 0, blk < last))(tell)
        lax.fori_loop(0, jnp.maximum(known - 1, 0), heard, 0)

    def stage_far(a, t):
        def own():
            far_in[a, blk, t] = by_head[t, table[0, near + far_number(a, blk)]]

        def other(target):
            slot = near + far_number(a, target)
            stage[slot, t] = by_head[t, table[0, slot]]

        other_far(a, other)
        if_far(a, blk, own)

    def stage_near(a, t):
        def own():
            near_in[a, line, t] = by_head[t, table[0, near_number(a, line)]]

        def other(target):
            slot = near_number(a, target)
            stage[slot, t] = by_head[t, table[0, slot]]

        other_near(a, other)
        if_near(a, line, own)

    def send_far(t, beside):
        def one(a, carry):
            def other(target):
                next_to = jnp.abs(target - blk) == 1
                pl.when(next_to if beside else jnp.logical_not(next_to))(
                    lambda: far_inward(a, t, target).start()
                )

            other_far(a, other)
            return carry

        lax.fori_loop(0, far_slots, one, 0)

    def send_near(t):
        def one(a, carry):
            other_near(a, lambda target: near_inward(a, t, target).start())
            return carry

        lax.fori_loop(0, near_slots, one, 0)

    def tensor(t, carry):
        def stage_one(a, carry):
            pl.when(a < far_slots)(lambda: stage_far(a, t))
            pl.when(a < near_slots)(lambda: stage_near(a, t))
            return carry

        @pl.when(t == 0)
        def _():
            split_heads(0, k_all)
            loads[0].wait()

        @pl.when(t == 1)
        def _():
            loads[1].wait()
            split_heads(1, v_all)

        @pl.when(t == 2)
        def _():
            loads[2].wait()
            split_heads(2, q_all)

        lax.fori_loop(0, max(near_slots, far_slots), stage_one, 0)

        @pl.when(t == 0)
        def _():
            pl.semaphore_wait(
                pltpu.get_barrier_semaphore(), line_count - 1 + below + above
            )

        send_far(t, True)
        send_near(t)

        @pl.when(t == 0)
        def _():
            pl.when(blk == 0)(functools.partial(clear, 0))
            pl.when(blk == last)(functools.partial(clear, 1))
            pass_on(1, below_sem)
            pass_on(-1, above_sem)

        send_far(t, False)
        return carry

    lax.fori_loop(0, 3, tensor, 0)

    def near_whole(a, carry):
        def whole():
            take(near_recv.at[a], near_in.at[a], line_count - 1)
            each_hop(lambda direction: hop(a, direction).start(), True)

        if_near(a, line, whole)
        return carry

    lax.fori_loop(0, near_slots, near_whole, 0)

    def finish_tile(scores, values):
        top = None
        for s in scores:
            top = s if top is None else jnp.maximum(top, s)
        row_top = jnp.max(top, axis=1, keepdims=True)
        total, accum = None, None
        for s, value in zip(scores, values):
            w = jnp.exp(s - row_top)
            part = jnp.dot(
                w.astype(jnp.bfloat16), value(), preferred_element_type=jnp.float32
            )
            total = w if total is None else total + w
            accum = part if accum is None else accum + part
        row_total = jnp.sum(total, axis=1, keepdims=True)
        return (accum / row_total).astype(jnp.bfloat16)

    def score(query, key, bits, place):
        s = lax.dot_general(
            query, key, (((1,), (1,)), ((), ())), preferred_element_type=jnp.float32
        )
        return s * score_scale + jnp.where((bits >> place) % 2 == 1, 0.0, NEG_FLOOR)

    def far_tile(a, source):
        bits = table[8 + source * line_count + line, near + far_number(a, blk)]
        query = far_in[a, source, 2]
        scores = [
            score(query, far_in[a, c, 0], bits, c * line_count + line) for c in range(n_blk)
        ]
        return finish_tile(
            scores, [lambda c=c: far_in[a, c, 1] for c in range(n_blk)]
        )

    def near_tile(a, source):
        bits = table[8 + first + source, near_number(a, line)] * (1 << line_count)
        query = near_in[a, source, 2]
        scores, values = [], []
        for f, tiles in ((1, near_in.at[a]), (0, near_side.at[a, 0]), (2, near_side.at[a, 1])):
            for c in range(line_count):
                scores.append(score(query, tiles[c, 0], bits, first + f * line_count + c))
                values.append(lambda tiles=tiles, c=c: tiles[c, 1])
        return finish_tile(scores, values)

    def work_through(a, count, peer, tile, outs, number, outward):
        def work(d, carry):
            result = tile(a, peer(d))

            @pl.when(d < count)
            def _():
                outs[a, peer(d)] = result

            @pl.when(d == count)
            def _():
                landed[number] = result

            @pl.when(d > 1)
            def _():
                outward(a, peer(d - 1)).start()

            return carry

        lax.fori_loop(1, count + 1, work, 0)

    def far_work(a, carry):
        take_far(far_send.at[a], far_in.at[a], a)

        def whole():
            take(far_recv.at[a], far_in.at[a], n_blk - 1)
            work_through(
                a, n_blk, blk_peer, far_tile, far_out, near + far_number(a, blk), far_outward
            )

        if_far(a, blk, whole)
        return carry

    lax.fori_loop(0, far_slots, far_work, 0)

    def near_work(a, carry):
        take_near(near_send.at[a], near_in.at[a], a)

        def whole():
            each_hop(lambda direction: hop(a, direction).wait_recv(), False)
            work_through(
                a, line_count, line_peer, near_tile, near_out, near_number(a, line), near_outward
            )

        if_near(a, line, whole)
        return carry

    lax.fori_loop(0, near_slots, near_work, 0)

    def finish_near(a, carry):
        def own():
            take(near_send.at[a], near_out.at[a], line_count - 1)
            each_hop(lambda direction: hop(a, direction).wait_send(), True)

        if_near(a, line, own)
        take_near(near_back.at[a], near_out.at[a], a)
        return carry

    def finish_far(a, carry):
        if_far(a, blk, lambda: take(far_send.at[a], far_out.at[a], n_blk - 1))
        take_far(far_back.at[a], far_out.at[a], a)
        return carry

    lax.fori_loop(0, near_slots, finish_near, 0)
    lax.fori_loop(0, far_slots, finish_far, 0)

    def restore(i, carry):
        for e in range(4):
            h = i * 4 + e
            out_ref[:, columns(h)] = landed[table[1, h]]
        return carry

    lax.fori_loop(0, HEADS // 4, restore, 0)


def split_exchange(sizes, near, collective_id, block_lists, table, keys, values, queries):
    n_blk, line_count = sizes[0], sizes[1] * sizes[2]
    rows, width = keys.shape
    near_slots = -(-near // line_count)
    far_slots = -(-(HEADS - near) // n_blk)
    block = (rows, HEAD_DIM)
    vmem = pl.BlockSpec(memory_space=pltpu.VMEM)
    anywhere = pl.BlockSpec(memory_space=pl.ANY)
    dma = pltpu.SemaphoreType.DMA

    def buffer(*lead):
        return pltpu.VMEM(lead + block, jnp.bfloat16)

    return pl.pallas_call(
        functools.partial(split_kernel, sizes, near),
        out_shape=jax.ShapeDtypeStruct((rows, width), jnp.bfloat16),
        in_specs=[anywhere, vmem, anywhere, anywhere],
        out_specs=vmem,
        scratch_shapes=[
            pltpu.SMEM(table.shape, jnp.int32),
            pltpu.VMEM((rows, width), jnp.bfloat16),
            pltpu.VMEM((rows, width), jnp.bfloat16),
            buffer(3, HEADS),
            buffer(HEADS, 3),
            buffer(near_slots, line_count, 3),
            buffer(near_slots, 2, line_count, 2),
            buffer(near_slots, line_count),
            buffer(far_slots, n_blk, 3),
            buffer(far_slots, n_blk),
            buffer(HEADS),
            dma((3,)),
            pltpu.SemaphoreType.REGULAR,
            pltpu.SemaphoreType.REGULAR,
            dma((near_slots,)),
            dma((near_slots,)),
            dma((near_slots,)),
            dma((near_slots, 2)),
            dma((near_slots, 2)),
            dma((far_slots,)),
            dma((far_slots,)),
            dma((far_slots,)),
        ],
        compiler_params=pltpu.CompilerParams(
            collective_id=collective_id, has_side_effects=True
        ),
    )(table, keys, values, queries)


def sort_kernel(frames, line_count, entries, lists_hbm, k_hbm, table, choice, k_all, lists_ref,
                sems):
    lists_load = pltpu.make_async_copy(lists_hbm, lists_ref, sems.at[0])
    load = pltpu.make_async_copy(k_hbm, k_all, sems.at[1])
    lists_load.start()
    load.start()
    lists_load.wait()
    ids = lists_ref[...]
    steps, heads = ids.shape
    tiles = steps // entries
    per_frame = steps // frames
    away = None
    for f in range(frames):
        part = ids[f * per_frame : (f + 1) * per_frame]
        outside = jnp.logical_or(part < (f - 1) * line_count, part >= (f + 2) * line_count)
        found = jnp.max(jnp.where(outside, 1, 0), axis=0, keepdims=True)
        away = found if away is None else jnp.maximum(away, found)
    row = lax.broadcasted_iota(jnp.int32, (heads, heads), 0)
    col = lax.broadcasted_iota(jnp.int32, (heads, heads), 1)
    away_col = jnp.broadcast_to(away, (heads, heads))
    away_row = jnp.broadcast_to(
        jnp.sum(jnp.where(row == col, away_col, 0), axis=1, keepdims=True), (heads, heads)
    )
    same = away_row == away_col
    ahead = jnp.where(same, jnp.where(row < col, 1, 0), away_col)
    place = jnp.sum(ahead, axis=0, keepdims=True)
    behind = jnp.where(same, jnp.where(col < row, 1, 0), away_row)
    place_of_row = jnp.sum(behind, axis=1, keepdims=True)
    perm = jnp.sum(
        jnp.where(jnp.broadcast_to(place_of_row, (heads, heads)) == col, row, 0),
        axis=0, keepdims=True,
    )
    table[0:1, 0:heads] = perm
    table[1:2, 0:heads] = place
    bits = None
    for e in range(entries):
        bit = jnp.left_shift(1, lists_ref[pl.ds(e, tiles, stride=entries), :])
        bits = bit if bits is None else jnp.bitwise_or(bits, bit)
    picks = jnp.where(jnp.broadcast_to(place, (heads, heads)) == row, 1.0, 0.0).astype(jnp.bfloat16)
    low, high = [
        lax.dot_general(
            part.astype(jnp.float32).astype(jnp.bfloat16), picks, (((1,), (1,)), ((), ())),
            preferred_element_type=jnp.float32,
        ).astype(jnp.int32)
        for part in (jnp.bitwise_and(bits, 255), jnp.right_shift(bits, 8))
    ]
    table[8 : 8 + tiles, 0:heads] = low + high * 256
    near = heads - jnp.sum(away.astype(jnp.float32)).astype(jnp.int32)
    least, most = EXACT_COUNTS[0], EXACT_COUNTS[-1]
    known = jnp.logical_and(near >= least, near <= most)
    choice[0] = jnp.where(known, near - least, most - least + 1)
    load.wait()


def sort_heads(line_count, keys, block_lists):
    heads, tiles, entries = block_lists.shape
    by_row = jnp.transpose(block_lists, (1, 2, 0)).reshape(tiles * entries, heads)
    vmem = pl.BlockSpec(memory_space=pltpu.VMEM)
    return pl.pallas_call(
        functools.partial(sort_kernel, tiles // line_count, line_count, entries),
        out_shape=(
            jax.ShapeDtypeStruct((8 + tiles, 128), jnp.int32),
            jax.ShapeDtypeStruct((1,), jnp.int32),
            jax.ShapeDtypeStruct(keys.shape, jnp.bfloat16),
        ),
        in_specs=[pl.BlockSpec(memory_space=pl.ANY)] * 2,
        out_specs=(vmem, pl.BlockSpec(memory_space=pltpu.SMEM), vmem),
        scratch_shapes=[pltpu.VMEM(by_row.shape, jnp.int32), pltpu.SemaphoreType.DMA((2,))],
    )(by_row, keys)


def solution(mesh):
    sizes = tuple(mesh.shape[axis] for axis in ("blk", "head", "sub"))
    line_count = sizes[1] * sizes[2]
    count = sizes[0] * line_count

    def body(queries, keys, values, block_lists):
        fits = queries.shape[0] == TILE and HEADS % count == 0 and count <= 16
        if not fits or block_lists.shape[1] != count:
            return per_device(queries, keys, values, block_lists)
        table, choice, held = sort_heads(line_count, keys, block_lists)
        branches = [
            functools.partial(split_exchange, sizes, n, number)
            for number, n in enumerate(EXACT_COUNTS)
        ]
        branches.append(functools.partial(general_exchange, sizes, len(EXACT_COUNTS)))
        return lax.switch(choice[0], branches, block_lists, table, held, values, queries)

    spec = P(("grp", "blk", "head", "sub"), None)
    return jax.shard_map(
        body, mesh=mesh, in_specs=(spec, spec, spec, P()), out_specs=spec, check_vma=False
    )
```

```python
import functools
import math

import jax
import jax.numpy as jnp
from jax import lax
from jax.experimental import pallas as pl
from jax.experimental.pallas import tpu as pltpu
from jax.sharding import PartitionSpec as P

HEADS = 32
HEAD_DIM = 128
TILE = 128


NEG_FLOOR = -1e30


def query_rows(block_lists, first_head, heads_here, query_tokens):
    tile_ids = jnp.arange(block_lists.shape[1], dtype=jnp.int32)
    lists_local = lax.dynamic_slice_in_dim(block_lists, first_head, heads_here, 0)
    tile_mask = jnp.any(lists_local[:, :, :, None] == tile_ids, axis=2).astype(jnp.bfloat16)
    query_onehot = ((query_tokens // TILE)[:, None] == tile_ids[None, :]).astype(jnp.bfloat16)
    listed = jnp.einsum("qi,hij->hqj", query_onehot, tile_mask, preferred_element_type=jnp.float32)
    return listed.astype(jnp.bfloat16)


def attend_block(state_now, key_block, value_block, allowed, query_local, score_scale):
    top_old, total_old, accum_old = state_now
    scores = (
        jnp.einsum("qhd,khd->hqk", query_local, key_block, preferred_element_type=jnp.float32)
        * score_scale
    )
    top_new = jnp.maximum(top_old, jnp.max(jnp.where(allowed, scores, NEG_FLOOR), axis=2))
    factor = jnp.exp(top_old - top_new)
    weights = jnp.where(allowed, jnp.exp(scores - top_new[:, :, None]), 0.0)
    total_new = total_old * factor + jnp.sum(weights, axis=2)
    product = jnp.einsum(
        "hqk,khd->qhd",
        weights.astype(jnp.bfloat16),
        value_block,
        preferred_element_type=jnp.float32,
    )
    accum_new = accum_old * jnp.transpose(factor)[:, :, None] + product
    return (top_new, total_new, accum_new)


def make_step(query_local, listed_rows, key_token, block_len, tile_total):
    score_scale = 1.0 / math.sqrt(HEAD_DIM)
    tile_ids = jnp.arange(tile_total, dtype=jnp.int32)

    def fold_step(state_now, piece, first_row):
        key_piece, value_piece = piece
        block_count = key_piece.shape[0] // block_len

        def one_block(block_index, state_in):
            key_block = lax.dynamic_slice_in_dim(key_piece, block_index * block_len, block_len, 0)
            value_block = lax.dynamic_slice_in_dim(
                value_piece, block_index * block_len, block_len, 0
            )
            positions = block_index * block_len + jnp.arange(block_len, dtype=jnp.int32)
            key_tiles = key_token(positions) // TILE
            key_onehot = (tile_ids[:, None] == key_tiles[None, :]).astype(jnp.bfloat16)
            allowed = (
                jnp.einsum(
                    "hqj,jk->hqk", listed_rows, key_onehot, preferred_element_type=jnp.float32
                )
                > 0.5
            )
            result = attend_block(
                state_in, key_block, value_block, allowed, query_local, score_scale
            )
            return result

        return lax.fori_loop(0, block_count, one_block, state_now)

    return fold_step


def start_state(heads_here, block_len):
    top_all = jnp.full((heads_here, block_len), NEG_FLOOR, jnp.float32)
    total_all = jnp.zeros((heads_here, block_len), jnp.float32)
    accum_all = jnp.zeros((block_len, heads_here, HEAD_DIM), jnp.float32)
    return (top_all, total_all, accum_all)


def normalize(state_end):
    top_all, total_all, accum_all = state_end
    return (accum_all / jnp.transpose(total_all)[:, :, None]).astype(jnp.bfloat16)


def per_device(queries, keys, values, block_lists):
    row_count, col_count = queries.shape
    n_head = lax.axis_size("head")
    n_sub = lax.axis_size("sub")
    blk_index = lax.axis_index("blk")
    head_index = lax.axis_index("head")
    sub_index = lax.axis_index("sub")
    tile_total = block_lists.shape[1]
    heads_here = HEADS // (n_head * n_sub)
    block_len = row_count * n_head * n_sub

    def inward(tensor):
        return tensor.reshape(1, 1, row_count, n_head, n_sub, heads_here * HEAD_DIM)

    query_six, keys_six, values_six = (
        lax.all_to_all(
            lax.all_to_all(inward(queries), "head", split_axis=3, concat_axis=1, tiled=True),
            "sub",
            split_axis=4,
            concat_axis=0,
            tiled=True,
        ),
        lax.all_to_all(
            lax.all_to_all(inward(keys), "head", split_axis=3, concat_axis=1, tiled=True),
            "sub",
            split_axis=4,
            concat_axis=0,
            tiled=True,
        ),
        lax.all_to_all(
            lax.all_to_all(inward(values), "head", split_axis=3, concat_axis=1, tiled=True),
            "sub",
            split_axis=4,
            concat_axis=0,
            tiled=True,
        ),
    )
    query_local = query_six.reshape(block_len, heads_here, HEAD_DIM)
    keys_local = keys_six.reshape(block_len, heads_here, HEAD_DIM)
    values_local = values_six.reshape(block_len, heads_here, HEAD_DIM)

    def key_token(positions):
        source_dev = positions // block_len
        within = positions % block_len
        sub_source = within // (n_head * row_count)
        head_source = within // row_count % n_head
        offset = within % row_count
        return ((source_dev * n_head + head_source) * n_sub + sub_source) * row_count + offset

    query_tokens = key_token(blk_index * block_len + jnp.arange(block_len, dtype=jnp.int32))
    first_head = (head_index * n_sub + sub_index) * heads_here
    listed_rows = query_rows(block_lists, first_head, heads_here, query_tokens)
    fold_step = make_step(query_local, listed_rows, key_token, block_len, tile_total)
    state_end = fold_step(
        start_state(heads_here, block_len),
        (
            lax.all_gather(keys_local, "blk", axis=0, tiled=True),
            lax.all_gather(values_local, "blk", axis=0, tiled=True),
        ),
        jnp.int32(0),
    )
    result_rows = normalize(state_end)
    attended = result_rows.reshape(n_sub, n_head, row_count, 1, 1, heads_here * HEAD_DIM)
    returned = lax.all_to_all(
        lax.all_to_all(attended, "head", split_axis=1, concat_axis=3, tiled=True),
        "sub",
        split_axis=0,
        concat_axis=4,
        tiled=True,
    )
    return returned.reshape(row_count, col_count)


EXACT_COUNTS = tuple(range(10, 23))


def rank_of(rank, n_head, n_sub):
    line_count = n_head * n_sub
    return {
        "blk": rank // line_count,
        "head": rank // n_sub % n_head,
        "sub": rank % n_sub,
    }


def remote_copy(sizes, src, dst, send, recv, rank):
    return pltpu.make_async_remote_copy(
        src_ref=src,
        dst_ref=dst,
        send_sem=send,
        recv_sem=recv,
        device_id=rank_of(rank, sizes[1], sizes[2]),
        device_id_type=pl.DeviceIdType.MESH,
    )


def greet(sizes, rank):
    pl.semaphore_signal(
        pltpu.get_barrier_semaphore(), inc=1,
        device_id=rank_of(rank, sizes[1], sizes[2]),
        device_id_type=pl.DeviceIdType.MESH,
    )


def attend_tile(ids, query, buf):
    score_scale = 1.0 / math.sqrt(HEAD_DIM)
    scores, top = [], None
    for tile in ids:
        s = lax.dot_general(
            query, buf[0, tile], (((1,), (1,)), ((), ())), preferred_element_type=jnp.float32
        ) * score_scale
        scores.append(s)
        top = s if top is None else jnp.maximum(top, s)
    row_top = jnp.max(top, axis=1, keepdims=True)
    total, accum = None, None
    for e, tile in enumerate(ids):
        w = jnp.exp(scores[e] - row_top)
        if e:
            repeat = tile == ids[0]
            for f in range(1, e):
                repeat = jnp.logical_or(repeat, tile == ids[f])
            w = w * jnp.where(repeat, 0.0, 1.0)
        part = jnp.dot(
            w.astype(jnp.bfloat16), buf[1, tile], preferred_element_type=jnp.float32
        )
        total = w if total is None else total + w
        accum = part if accum is None else accum + part
    row_total = jnp.sum(total, axis=1, keepdims=True)
    return (accum / row_total).astype(jnp.bfloat16)


def general_kernel(sizes, entries, stage, list_rows, landed, lists, list_sem, *scratch):
    n_blk, n_head, n_sub = sizes
    line_count = n_head * n_sub
    count = n_blk * line_count
    heads_here = HEADS // count
    far_in = scratch[:heads_here]
    far_out = scratch[heads_here : 2 * heads_here]
    send_sem, recv_sem, local_sem = scratch[2 * heads_here :]
    line = lax.axis_index("head") * n_sub + lax.axis_index("sub")
    me = lax.axis_index("blk") * line_count + line

    def peer(d):
        return (me + d) % count

    def inward(t, a, target, sender):
        return remote_copy(
            sizes, stage.at[t, a * count + target], far_in[a].at[t, sender],
            send_sem.at[t, a, target], recv_sem.at[t, a, sender], target,
        )

    def outward(a, target, sender):
        return remote_copy(
            sizes, far_out[a].at[target], landed.at[a * count + sender],
            send_sem.at[3, a, target], recv_sem.at[3, a, sender], target,
        )

    def own_in(t, a):
        return pltpu.make_async_copy(
            stage.at[t, a * count + me], far_in[a].at[t, me], local_sem.at[t, a]
        )

    def own_out(a):
        return pltpu.make_async_copy(
            far_out[a].at[me], landed.at[a * count + me], local_sem.at[3, a]
        )

    def own_list(a):
        return pltpu.make_async_copy(
            list_rows.at[a * count + me], lists.at[a], list_sem.at[a]
        )

    def greet_all(d, carry):
        greet(sizes, peer(d))
        return carry

    lax.fori_loop(1, count, greet_all, 0)
    for a in range(heads_here):
        own_list(a).start()
    pl.semaphore_wait(pltpu.get_barrier_semaphore(), count - 1)

    for a in range(heads_here):
        def send_in(d, carry, a=a):
            for t in range(3):
                inward(t, a, peer(d), me).start()
            return carry

        lax.fori_loop(1, count, send_in, 0)
        for t in range(3):
            own_in(t, a).start()

    for a in range(heads_here):
        for t in range(3):
            own_in(t, a).wait()

        def arrive(d, carry, a=a):
            for t in range(3):
                inward(t, a, me, peer(d)).wait_recv()
            return carry

        lax.fori_loop(1, count, arrive, 0)
        own_list(a).wait()

        def one(i, a=a):
            ids = [lists[a, i * entries + e] for e in range(entries)]
            far_out[a][i] = attend_tile(ids, far_in[a][2, i], far_in[a])

        def work(d, carry, a=a, one=one):
            one(peer(d))

            @pl.when(d > 1)
            def _():
                outward(a, peer(d - 1), me).start()

            return carry

        lax.fori_loop(1, count + 1, work, 0)
        own_out(a).start()

    for a in range(heads_here):
        own_out(a).wait()

        def finish(d, carry, a=a):
            for t in range(3):
                inward(t, a, peer(d), me).wait_send()
            outward(a, peer(d), me).wait_send()
            outward(a, me, peer(d)).wait_recv()
            return carry

        lax.fori_loop(1, count, finish, 0)


def general_exchange(sizes, collective_id, block_lists, table, keys, values, queries):
    count = sizes[0] * sizes[1] * sizes[2]
    rows = keys.shape[0]
    stage = jnp.stack([keys, values, queries]).reshape(3, rows, HEADS, HEAD_DIM)
    stage = jnp.swapaxes(stage, 1, 2)
    block = (rows, HEAD_DIM)
    heads_here = HEADS // count
    list_rows = block_lists.reshape(HEADS, -1)
    anywhere = pl.BlockSpec(memory_space=pl.ANY)
    dma = pltpu.SemaphoreType.DMA
    scratch = [pltpu.SMEM((heads_here, list_rows.shape[1]), jnp.int32), dma((heads_here,))]
    scratch += [pltpu.VMEM((3, count) + block, jnp.bfloat16)] * heads_here
    scratch += [pltpu.VMEM((count,) + block, jnp.bfloat16)] * heads_here
    scratch += [dma((4, heads_here, count))] * 2 + [dma((4, heads_here))]
    landed = pl.pallas_call(
        functools.partial(general_kernel, sizes, block_lists.shape[2]),
        out_shape=jax.ShapeDtypeStruct((HEADS,) + block, jnp.bfloat16),
        in_specs=[anywhere, anywhere],
        out_specs=anywhere,
        scratch_shapes=scratch,
        compiler_params=pltpu.CompilerParams(
            collective_id=collective_id, has_side_effects=True
        ),
    )(stage, list_rows)
    return jnp.swapaxes(landed, 0, 1).reshape(rows, HEADS * HEAD_DIM)


def split_kernel(sizes, near, table_ref, k_all, v_hbm, q_hbm, out_ref, table, v_all, q_all, by_head, stage, near_in, near_side,
                 near_out, far_in, far_out, landed, local_sem, below_sem, above_sem, near_send, near_recv, near_back,
                 hop_send, hop_recv, far_send, far_recv, far_back):
    n_blk, n_head, n_sub = sizes
    line_count = n_head * n_sub
    far = HEADS - near
    near_slots = -(-near // line_count)
    far_slots = -(-far // n_blk)
    score_scale = 1.0 / math.sqrt(HEAD_DIM)

    blk, sub = lax.axis_index("blk"), lax.axis_index("sub")
    line = lax.axis_index("head") * n_sub + sub
    first = blk * line_count

    def near_number(a, target_line):
        return a * line_count + target_line % n_sub * n_head + target_line // n_sub

    def far_number(a, target_blk):
        mirrored = target_blk + sub % 2 * (n_blk - 1 - 2 * target_blk)
        return a * n_blk + (mirrored + n_blk - 1) % n_blk

    def line_peer(d):
        return (line + d) % line_count

    def blk_peer(d):
        return (blk + d) % n_blk

    def if_near(a, target_line, action):
        pl.when(near_number(a, target_line) < near)(action)

    def if_far(a, target_blk, action):
        pl.when(far_number(a, target_blk) < far)(action)

    def each_other(count, peer, test, action):
        def one(d, carry):
            test(peer(d), lambda: action(peer(d)))
            return carry

        lax.fori_loop(1, count, one, 0)

    def other_far(a, action):
        each_other(n_blk, blk_peer, functools.partial(if_far, a), action)

    def other_near(a, action):
        each_other(line_count, line_peer, functools.partial(if_near, a), action)

    def take(sem, unit, pieces):
        if pieces:
            part = unit.at[pl.ds(0, pieces)]
            pltpu.make_async_copy(part, part, sem).wait()

    def take_others(sem, unit, a, own, total, count):
        rest = total % count
        if total >= count:
            pl.when(a < total // count)(lambda: take(sem, unit, count - 1))
        if rest:
            last = a == total // count
            pl.when(jnp.logical_and(last, own < total))(lambda: take(sem, unit, rest - 1))
            pl.when(jnp.logical_and(last, own >= total))(lambda: take(sem, unit, rest))

    def take_far(sem, unit, a):
        take_others(sem, unit, a, far_number(a, blk), far, n_blk)

    def take_near(sem, unit, a):
        take_others(sem, unit, a, near_number(a, line), near, line_count)

    def near_inward(a, t, target):
        return remote_copy(
            sizes, stage.at[near_number(a, target), t], near_in.at[a, line, t],
            near_send.at[a], near_recv.at[a], first + target,
        )

    def near_outward(a, target):
        return remote_copy(
            sizes, near_out.at[a, target], landed.at[near_number(a, line)],
            near_send.at[a], near_back.at[a], first + target,
        )

    def hop(a, direction):
        step = 1 - 2 * direction
        return remote_copy(
            sizes, near_in.at[a, :, pl.ds(0, 2)], near_side.at[a, direction],
            hop_send.at[a, direction], hop_recv.at[a, direction],
            (blk + n_blk + step) % n_blk * line_count + line,
        )

    def each_hop(action, sending):
        up, down = blk < n_blk - 1, blk > 0
        pl.when(up if sending else down)(functools.partial(action, 0))
        pl.when(down if sending else up)(functools.partial(action, 1))

    def far_inward(a, t, target):
        return remote_copy(
            sizes, stage.at[near + far_number(a, target), t], far_in.at[a, blk, t],
            far_send.at[a], far_recv.at[a], target * line_count + line,
        )

    def far_outward(a, target):
        return remote_copy(
            sizes, far_out.at[a, target], landed.at[near + far_number(a, blk)],
            far_send.at[a], far_back.at[a], target * line_count + line,
        )

    last = n_blk - 1
    below, above = (blk > 0).astype(jnp.int32), (blk < last).astype(jnp.int32)
    pl.when(blk < last)(lambda: greet(sizes, first + line_count + line))
    pl.when(blk > 0)(lambda: greet(sizes, first - line_count + line))
    for d in range(1, line_count):
        greet(sizes, first + line_peer(d))
    loads = [
        pltpu.make_async_copy(table_ref, table, local_sem.at[0]),
        pltpu.make_async_copy(v_hbm, v_all, local_sem.at[1]),
        pltpu.make_async_copy(q_hbm, q_all, local_sem.at[2]),
    ]
    for load in loads:
        load.start()

    def clear(side):
        def clear_tile(i, carry):
            near_side[i // line_count, side, i % line_count] = jnp.zeros(
                near_side.shape[3:], near_side.dtype
            )
            return carry

        lax.fori_loop(0, near_slots * line_count, clear_tile, 0)

    def columns(h):
        return pl.ds(pl.multiple_of(h * HEAD_DIM, HEAD_DIM), HEAD_DIM)

    def split_heads(t, source):
        def split_head(h, carry):
            by_head[t, h] = source[:, columns(h)]
            return carry

        lax.fori_loop(0, HEADS, split_head, 0)

    def tell(step, sem):
        pl.semaphore_signal(
            sem, inc=1,
            device_id=rank_of(first + step * line_count + line, n_head, n_sub),
            device_id_type=pl.DeviceIdType.MESH,
        )

    def pass_on(step, sem):
        def heard(e, carry):
            pl.semaphore_wait(sem, 1)
            pl.when(blk < last if step > 0 else blk > 0)(lambda: tell(step, sem))
            return carry

        known = blk if step > 0 else last - blk
        lax.fori_loop(0, jnp.maximum(known - 1, 0), heard, 0)

    def stage_far(a, t):
        def own():
            far_in[a, blk, t] = by_head[t, table[0, near + far_number(a, blk)]]

        def other(target):
            slot = near + far_number(a, target)
            stage[slot, t] = by_head[t, table[0, slot]]

        other_far(a, other)
        if_far(a, blk, own)

    def stage_near(a, t):
        def own():
            near_in[a, line, t] = by_head[t, table[0, near_number(a, line)]]

        def other(target):
            slot = near_number(a, target)
            stage[slot, t] = by_head[t, table[0, slot]]

        other_near(a, other)
        if_near(a, line, own)

    def send_far(t, beside):
        def one(a, carry):
            def other(target):
                next_to = jnp.abs(target - blk) == 1
                pl.when(next_to if beside else jnp.logical_not(next_to))(
                    lambda: far_inward(a, t, target).start()
                )

            other_far(a, other)
            return carry

        lax.fori_loop(0, far_slots, one, 0)

    def send_near(t):
        def one(a, carry):
            other_near(a, lambda target: near_inward(a, t, target).start())
            return carry

        lax.fori_loop(0, near_slots, one, 0)

    def each_slot(slots, action, t):
        def one(a, carry):
            action(a, t)
            return carry

        lax.fori_loop(0, slots, one, 0)

    def tensor(t, carry):
        @pl.when(t == 0)
        def _():
            split_heads(0, k_all)
            loads[0].wait()

        @pl.when(t == 1)
        def _():
            loads[1].wait()
            split_heads(1, v_all)

        @pl.when(t == 2)
        def _():
            loads[2].wait()
            split_heads(2, q_all)

        each_slot(far_slots, stage_far, t)

        @pl.when(t == 0)
        def _():
            pl.semaphore_wait(
                pltpu.get_barrier_semaphore(), line_count - 1 + below + above
            )

            @pl.when(jnp.logical_and(blk > 0, blk < last))
            def _():
                tell(1, below_sem)
                tell(-1, above_sem)

        send_far(t, True)
        each_slot(near_slots, stage_near, t)
        send_near(t)

        @pl.when(t == 0)
        def _():
            pl.when(blk == 0)(functools.partial(clear, 0))
            pl.when(blk == last)(functools.partial(clear, 1))
            pass_on(1, below_sem)
            pass_on(-1, above_sem)

        send_far(t, False)
        return carry

    lax.fori_loop(0, 3, tensor, 0)

    def near_whole(a, carry):
        def whole():
            take(near_recv.at[a], near_in.at[a], line_count - 1)
            each_hop(lambda direction: hop(a, direction).start(), True)

        if_near(a, line, whole)
        return carry

    lax.fori_loop(0, near_slots, near_whole, 0)

    def attend_pair(query, bits, tiles):
        rows = query.shape[0] // len(bits)
        scores = [[] for _ in bits]
        for e in range(0, len(tiles), 2):
            some = tiles[e : e + 2]
            s = lax.dot_general(
                query, jnp.concatenate([tile[0]() for tile in some]), (((1,), (1,)), ((), ())),
                preferred_element_type=jnp.float32,
            ) * score_scale
            for half, mask in enumerate(bits):
                for c, (_, _, place) in enumerate(some):
                    part = s[half * rows : (half + 1) * rows, c * rows : (c + 1) * rows]
                    bias = jnp.where((mask >> place) % 2 == 1, 0.0, NEG_FLOOR)
                    scores[half].append(part + bias)
        tops = [
            jnp.max(functools.reduce(jnp.maximum, part), axis=1, keepdims=True) for part in scores
        ]
        totals, accum = [None] * len(bits), None
        for e in range(0, len(tiles), 2):
            some, weights = tiles[e : e + 2], []
            for half, top in enumerate(tops):
                wide = [jnp.exp(scores[half][e + c] - top) for c in range(len(some))]
                for w in wide:
                    totals[half] = w if totals[half] is None else totals[half] + w
                weights.append(jnp.concatenate([w.astype(jnp.bfloat16) for w in wide], axis=1))
            part = jnp.dot(
                jnp.concatenate(weights), jnp.concatenate([tile[1]() for tile in some]),
                preferred_element_type=jnp.float32,
            )
            accum = part if accum is None else accum + part
        return [
            (
                accum[half * rows : (half + 1) * rows] / jnp.sum(total, axis=1, keepdims=True)
            ).astype(jnp.bfloat16)
            for half, total in enumerate(totals)
        ]

    def pick(ref, c):
        return lambda: ref[c, 0], lambda: ref[c, 1]

    def far_pair(a, sources):
        number = near + far_number(a, blk)
        bits = [table[8 + source * line_count + line, number] for source in sources]
        query = jnp.concatenate([far_in[a, source, 2] for source in sources])
        held = far_in.at[a]
        return attend_pair(
            query, bits, [pick(held, c) + (c * line_count + line,) for c in range(n_blk)]
        )

    def near_pair(a, sources):
        number = near_number(a, line)
        bits = [table[8 + first + source, number] * (1 << line_count) for source in sources]
        query = jnp.concatenate([near_in[a, source, 2] for source in sources])
        tiles = []
        for f, held in ((1, near_in.at[a]), (0, near_side.at[a, 0]), (2, near_side.at[a, 1])):
            tiles += [
                pick(held, c) + (first + f * line_count + c,) for c in range(line_count)
            ]
        return attend_pair(query, bits, tiles)

    def work_through(a, count, peer, pair, outs, number, outward):
        def work(i, carry):
            d = 2 * i + 1
            results = pair(a, (peer(d), peer(d + 1)))

            @pl.when(i > 0)
            def _():
                outward(a, peer(d - 2)).start()
                outward(a, peer(d - 1)).start()

            outs[a, peer(d)] = results[0]

            @pl.when(d + 1 < count)
            def _():
                outs[a, peer(d + 1)] = results[1]

            @pl.when(d + 1 == count)
            def _():
                landed[number] = results[1]

            return carry

        lax.fori_loop(0, count // 2, work, 0)
        outward(a, peer(count - 1)).start()

    def far_work(a, carry):
        take_far(far_send.at[a], far_in.at[a], a)

        def whole():
            take(far_recv.at[a], far_in.at[a], n_blk - 1)
            work_through(
                a, n_blk, blk_peer, far_pair, far_out, near + far_number(a, blk), far_outward
            )

        if_far(a, blk, whole)
        return carry

    lax.fori_loop(0, far_slots, far_work, 0)

    def near_work(a, carry):
        take_near(near_send.at[a], near_in.at[a], a)

        def whole():
            each_hop(lambda direction: hop(a, direction).wait_recv(), False)
            work_through(
                a, line_count, line_peer, near_pair, near_out, near_number(a, line), near_outward
            )

        if_near(a, line, whole)
        return carry

    lax.fori_loop(0, near_slots, near_work, 0)

    def finish_near(a, carry):
        def own():
            take(near_send.at[a], near_out.at[a], line_count - 1)
            each_hop(lambda direction: hop(a, direction).wait_send(), True)

        if_near(a, line, own)
        take_near(near_back.at[a], near_out.at[a], a)
        return carry

    def finish_far(a, carry):
        if_far(a, blk, lambda: take(far_send.at[a], far_out.at[a], n_blk - 1))
        take_far(far_back.at[a], far_out.at[a], a)
        return carry

    lax.fori_loop(0, near_slots, finish_near, 0)
    lax.fori_loop(0, far_slots, finish_far, 0)

    def restore(i, carry):
        for e in range(4):
            h = i * 4 + e
            out_ref[:, columns(h)] = landed[table[1, h]]
        return carry

    lax.fori_loop(0, HEADS // 4, restore, 0)


def split_exchange(sizes, near, collective_id, block_lists, table, keys, values, queries):
    n_blk, line_count = sizes[0], sizes[1] * sizes[2]
    rows, width = keys.shape
    near_slots = -(-near // line_count)
    far_slots = -(-(HEADS - near) // n_blk)
    block = (rows, HEAD_DIM)
    vmem = pl.BlockSpec(memory_space=pltpu.VMEM)
    anywhere = pl.BlockSpec(memory_space=pl.ANY)
    dma = pltpu.SemaphoreType.DMA

    def buffer(*lead):
        return pltpu.VMEM(lead + block, jnp.bfloat16)

    return pl.pallas_call(
        functools.partial(split_kernel, sizes, near),
        out_shape=jax.ShapeDtypeStruct((rows, width), jnp.bfloat16),
        in_specs=[anywhere, vmem, anywhere, anywhere],
        out_specs=vmem,
        scratch_shapes=[
            pltpu.SMEM(table.shape, jnp.int32),
            pltpu.VMEM((rows, width), jnp.bfloat16),
            pltpu.VMEM((rows, width), jnp.bfloat16),
            buffer(3, HEADS),
            buffer(HEADS, 3),
            buffer(near_slots, line_count, 3),
            buffer(near_slots, 2, line_count, 2),
            buffer(near_slots, line_count),
            buffer(far_slots, n_blk, 3),
            buffer(far_slots, n_blk),
            buffer(HEADS),
            dma((3,)),
            pltpu.SemaphoreType.REGULAR,
            pltpu.SemaphoreType.REGULAR,
            dma((near_slots,)),
            dma((near_slots,)),
            dma((near_slots,)),
            dma((near_slots, 2)),
            dma((near_slots, 2)),
            dma((far_slots,)),
            dma((far_slots,)),
            dma((far_slots,)),
        ],
        compiler_params=pltpu.CompilerParams(
            collective_id=collective_id, has_side_effects=True
        ),
    )(table, keys, values, queries)


def sort_kernel(frames, line_count, entries, lists_hbm, k_hbm, table, choice, k_all, lists_ref,
                sems):
    lists_load = pltpu.make_async_copy(lists_hbm, lists_ref, sems.at[0])
    load = pltpu.make_async_copy(k_hbm, k_all, sems.at[1])
    lists_load.start()
    load.start()
    lists_load.wait()
    ids = lists_ref[...]
    steps, heads = ids.shape
    tiles = steps // entries
    per_frame = steps // frames
    away = None
    for f in range(frames):
        part = ids[f * per_frame : (f + 1) * per_frame]
        outside = jnp.logical_or(part < (f - 1) * line_count, part >= (f + 2) * line_count)
        found = jnp.max(jnp.where(outside, 1, 0), axis=0, keepdims=True)
        away = found if away is None else jnp.maximum(away, found)
    row = lax.broadcasted_iota(jnp.int32, (heads, heads), 0)
    col = lax.broadcasted_iota(jnp.int32, (heads, heads), 1)
    away_col = jnp.broadcast_to(away, (heads, heads))
    away_row = jnp.broadcast_to(
        jnp.sum(jnp.where(row == col, away_col, 0), axis=1, keepdims=True), (heads, heads)
    )
    same = away_row == away_col
    ahead = jnp.where(same, jnp.where(row < col, 1, 0), away_col)
    place = jnp.sum(ahead, axis=0, keepdims=True)
    behind = jnp.where(same, jnp.where(col < row, 1, 0), away_row)
    place_of_row = jnp.sum(behind, axis=1, keepdims=True)
    perm = jnp.sum(
        jnp.where(jnp.broadcast_to(place_of_row, (heads, heads)) == col, row, 0),
        axis=0, keepdims=True,
    )
    table[0:1, 0:heads] = perm
    table[1:2, 0:heads] = place
    bits = None
    for e in range(entries):
        bit = jnp.left_shift(1, lists_ref[pl.ds(e, tiles, stride=entries), :])
        bits = bit if bits is None else jnp.bitwise_or(bits, bit)
    picks = jnp.where(jnp.broadcast_to(place, (heads, heads)) == row, 1.0, 0.0).astype(jnp.bfloat16)
    low, high = [
        lax.dot_general(
            part.astype(jnp.float32).astype(jnp.bfloat16), picks, (((1,), (1,)), ((), ())),
            preferred_element_type=jnp.float32,
        ).astype(jnp.int32)
        for part in (jnp.bitwise_and(bits, 255), jnp.right_shift(bits, 8))
    ]
    table[8 : 8 + tiles, 0:heads] = low + high * 256
    near = heads - jnp.sum(away.astype(jnp.float32)).astype(jnp.int32)
    least, most = EXACT_COUNTS[0], EXACT_COUNTS[-1]
    known = jnp.logical_and(near >= least, near <= most)
    choice[0] = jnp.where(known, near - least, most - least + 1)
    load.wait()


def sort_heads(line_count, keys, block_lists):
    heads, tiles, entries = block_lists.shape
    by_row = jnp.transpose(block_lists, (1, 2, 0)).reshape(tiles * entries, heads)
    vmem = pl.BlockSpec(memory_space=pltpu.VMEM)
    return pl.pallas_call(
        functools.partial(sort_kernel, tiles // line_count, line_count, entries),
        out_shape=(
            jax.ShapeDtypeStruct((8 + tiles, 128), jnp.int32),
            jax.ShapeDtypeStruct((1,), jnp.int32),
            jax.ShapeDtypeStruct(keys.shape, jnp.bfloat16),
        ),
        in_specs=[pl.BlockSpec(memory_space=pl.ANY)] * 2,
        out_specs=(vmem, pl.BlockSpec(memory_space=pltpu.SMEM), vmem),
        scratch_shapes=[pltpu.VMEM(by_row.shape, jnp.int32), pltpu.SemaphoreType.DMA((2,))],
    )(by_row, keys)


def solution(mesh):
    sizes = tuple(mesh.shape[axis] for axis in ("blk", "head", "sub"))
    line_count = sizes[1] * sizes[2]
    count = sizes[0] * line_count

    def body(queries, keys, values, block_lists):
        fits = queries.shape[0] == TILE and HEADS % count == 0 and count <= 16 and sizes[0] % 2 == 0 and line_count % 2 == 0
        if not fits or block_lists.shape[1] != count:
            return per_device(queries, keys, values, block_lists)
        table, choice, held = sort_heads(line_count, keys, block_lists)
        branches = [
            functools.partial(split_exchange, sizes, n, number)
            for number, n in enumerate(EXACT_COUNTS)
        ]
        branches.append(functools.partial(general_exchange, sizes, len(EXACT_COUNTS)))
        return lax.switch(choice[0], branches, block_lists, table, held, values, queries)

    spec = P(("grp", "blk", "head", "sub"), None)
    return jax.shard_map(
        body, mesh=mesh, in_specs=(spec, spec, spec, P()), out_specs=spec, check_vma=False
    )
```

```python
import functools
import math

import jax
import jax.numpy as jnp
from jax import lax
from jax.experimental import pallas as pl
from jax.experimental.pallas import tpu as pltpu
from jax.sharding import PartitionSpec as P

HEADS = 32
HEAD_DIM = 128
TILE = 128


NEG_FLOOR = -1e30


def query_rows(block_lists, first_head, heads_here, query_tokens):
    tile_ids = jnp.arange(block_lists.shape[1], dtype=jnp.int32)
    lists_local = lax.dynamic_slice_in_dim(block_lists, first_head, heads_here, 0)
    tile_mask = jnp.any(lists_local[:, :, :, None] == tile_ids, axis=2).astype(jnp.bfloat16)
    query_onehot = ((query_tokens // TILE)[:, None] == tile_ids[None, :]).astype(jnp.bfloat16)
    listed = jnp.einsum("qi,hij->hqj", query_onehot, tile_mask, preferred_element_type=jnp.float32)
    return listed.astype(jnp.bfloat16)


def attend_block(state_now, key_block, value_block, allowed, query_local, score_scale):
    top_old, total_old, accum_old = state_now
    scores = (
        jnp.einsum("qhd,khd->hqk", query_local, key_block, preferred_element_type=jnp.float32)
        * score_scale
    )
    top_new = jnp.maximum(top_old, jnp.max(jnp.where(allowed, scores, NEG_FLOOR), axis=2))
    factor = jnp.exp(top_old - top_new)
    weights = jnp.where(allowed, jnp.exp(scores - top_new[:, :, None]), 0.0)
    total_new = total_old * factor + jnp.sum(weights, axis=2)
    product = jnp.einsum(
        "hqk,khd->qhd",
        weights.astype(jnp.bfloat16),
        value_block,
        preferred_element_type=jnp.float32,
    )
    accum_new = accum_old * jnp.transpose(factor)[:, :, None] + product
    return (top_new, total_new, accum_new)


def make_step(query_local, listed_rows, key_token, block_len, tile_total):
    score_scale = 1.0 / math.sqrt(HEAD_DIM)
    tile_ids = jnp.arange(tile_total, dtype=jnp.int32)

    def fold_step(state_now, piece, first_row):
        key_piece, value_piece = piece
        block_count = key_piece.shape[0] // block_len

        def one_block(block_index, state_in):
            key_block = lax.dynamic_slice_in_dim(key_piece, block_index * block_len, block_len, 0)
            value_block = lax.dynamic_slice_in_dim(
                value_piece, block_index * block_len, block_len, 0
            )
            positions = block_index * block_len + jnp.arange(block_len, dtype=jnp.int32)
            key_tiles = key_token(positions) // TILE
            key_onehot = (tile_ids[:, None] == key_tiles[None, :]).astype(jnp.bfloat16)
            allowed = (
                jnp.einsum(
                    "hqj,jk->hqk", listed_rows, key_onehot, preferred_element_type=jnp.float32
                )
                > 0.5
            )
            result = attend_block(
                state_in, key_block, value_block, allowed, query_local, score_scale
            )
            return result

        return lax.fori_loop(0, block_count, one_block, state_now)

    return fold_step


def start_state(heads_here, block_len):
    top_all = jnp.full((heads_here, block_len), NEG_FLOOR, jnp.float32)
    total_all = jnp.zeros((heads_here, block_len), jnp.float32)
    accum_all = jnp.zeros((block_len, heads_here, HEAD_DIM), jnp.float32)
    return (top_all, total_all, accum_all)


def normalize(state_end):
    top_all, total_all, accum_all = state_end
    return (accum_all / jnp.transpose(total_all)[:, :, None]).astype(jnp.bfloat16)


def per_device(queries, keys, values, block_lists):
    row_count, col_count = queries.shape
    n_head = lax.axis_size("head")
    n_sub = lax.axis_size("sub")
    blk_index = lax.axis_index("blk")
    head_index = lax.axis_index("head")
    sub_index = lax.axis_index("sub")
    tile_total = block_lists.shape[1]
    heads_here = HEADS // (n_head * n_sub)
    block_len = row_count * n_head * n_sub

    def inward(tensor):
        return tensor.reshape(1, 1, row_count, n_head, n_sub, heads_here * HEAD_DIM)

    query_six, keys_six, values_six = (
        lax.all_to_all(
            lax.all_to_all(inward(queries), "head", split_axis=3, concat_axis=1, tiled=True),
            "sub",
            split_axis=4,
            concat_axis=0,
            tiled=True,
        ),
        lax.all_to_all(
            lax.all_to_all(inward(keys), "head", split_axis=3, concat_axis=1, tiled=True),
            "sub",
            split_axis=4,
            concat_axis=0,
            tiled=True,
        ),
        lax.all_to_all(
            lax.all_to_all(inward(values), "head", split_axis=3, concat_axis=1, tiled=True),
            "sub",
            split_axis=4,
            concat_axis=0,
            tiled=True,
        ),
    )
    query_local = query_six.reshape(block_len, heads_here, HEAD_DIM)
    keys_local = keys_six.reshape(block_len, heads_here, HEAD_DIM)
    values_local = values_six.reshape(block_len, heads_here, HEAD_DIM)

    def key_token(positions):
        source_dev = positions // block_len
        within = positions % block_len
        sub_source = within // (n_head * row_count)
        head_source = within // row_count % n_head
        offset = within % row_count
        return ((source_dev * n_head + head_source) * n_sub + sub_source) * row_count + offset

    query_tokens = key_token(blk_index * block_len + jnp.arange(block_len, dtype=jnp.int32))
    first_head = (head_index * n_sub + sub_index) * heads_here
    listed_rows = query_rows(block_lists, first_head, heads_here, query_tokens)
    fold_step = make_step(query_local, listed_rows, key_token, block_len, tile_total)
    state_end = fold_step(
        start_state(heads_here, block_len),
        (
            lax.all_gather(keys_local, "blk", axis=0, tiled=True),
            lax.all_gather(values_local, "blk", axis=0, tiled=True),
        ),
        jnp.int32(0),
    )
    result_rows = normalize(state_end)
    attended = result_rows.reshape(n_sub, n_head, row_count, 1, 1, heads_here * HEAD_DIM)
    returned = lax.all_to_all(
        lax.all_to_all(attended, "head", split_axis=1, concat_axis=3, tiled=True),
        "sub",
        split_axis=0,
        concat_axis=4,
        tiled=True,
    )
    return returned.reshape(row_count, col_count)


EXACT_COUNTS = tuple(range(10, 23))


def rank_of(rank, n_head, n_sub):
    line_count = n_head * n_sub
    return {
        "blk": rank // line_count,
        "head": rank // n_sub % n_head,
        "sub": rank % n_sub,
    }


def remote_copy(sizes, src, dst, send, recv, rank):
    return pltpu.make_async_remote_copy(
        src_ref=src,
        dst_ref=dst,
        send_sem=send,
        recv_sem=recv,
        device_id=rank_of(rank, sizes[1], sizes[2]),
        device_id_type=pl.DeviceIdType.MESH,
    )


def greet(sizes, rank):
    pl.semaphore_signal(
        pltpu.get_barrier_semaphore(), inc=1,
        device_id=rank_of(rank, sizes[1], sizes[2]),
        device_id_type=pl.DeviceIdType.MESH,
    )


def attend_tile(ids, query, buf):
    score_scale = 1.0 / math.sqrt(HEAD_DIM)
    scores, top = [], None
    for tile in ids:
        s = lax.dot_general(
            query, buf[0, tile], (((1,), (1,)), ((), ())), preferred_element_type=jnp.float32
        ) * score_scale
        scores.append(s)
        top = s if top is None else jnp.maximum(top, s)
    row_top = jnp.max(top, axis=1, keepdims=True)
    total, accum = None, None
    for e, tile in enumerate(ids):
        w = jnp.exp(scores[e] - row_top)
        if e:
            repeat = tile == ids[0]
            for f in range(1, e):
                repeat = jnp.logical_or(repeat, tile == ids[f])
            w = w * jnp.where(repeat, 0.0, 1.0)
        part = jnp.dot(
            w.astype(jnp.bfloat16), buf[1, tile], preferred_element_type=jnp.float32
        )
        total = w if total is None else total + w
        accum = part if accum is None else accum + part
    row_total = jnp.sum(total, axis=1, keepdims=True)
    return (accum / row_total).astype(jnp.bfloat16)


def general_kernel(sizes, entries, stage, list_rows, landed, lists, list_sem, *scratch):
    n_blk, n_head, n_sub = sizes
    line_count = n_head * n_sub
    count = n_blk * line_count
    heads_here = HEADS // count
    far_in = scratch[:heads_here]
    far_out = scratch[heads_here : 2 * heads_here]
    send_sem, recv_sem, local_sem = scratch[2 * heads_here :]
    line = lax.axis_index("head") * n_sub + lax.axis_index("sub")
    me = lax.axis_index("blk") * line_count + line

    def peer(d):
        return (me + d) % count

    def inward(t, a, target, sender):
        return remote_copy(
            sizes, stage.at[t, a * count + target], far_in[a].at[t, sender],
            send_sem.at[t, a, target], recv_sem.at[t, a, sender], target,
        )

    def outward(a, target, sender):
        return remote_copy(
            sizes, far_out[a].at[target], landed.at[a * count + sender],
            send_sem.at[3, a, target], recv_sem.at[3, a, sender], target,
        )

    def own_in(t, a):
        return pltpu.make_async_copy(
            stage.at[t, a * count + me], far_in[a].at[t, me], local_sem.at[t, a]
        )

    def own_out(a):
        return pltpu.make_async_copy(
            far_out[a].at[me], landed.at[a * count + me], local_sem.at[3, a]
        )

    def own_list(a):
        return pltpu.make_async_copy(
            list_rows.at[a * count + me], lists.at[a], list_sem.at[a]
        )

    def greet_all(d, carry):
        greet(sizes, peer(d))
        return carry

    lax.fori_loop(1, count, greet_all, 0)
    for a in range(heads_here):
        own_list(a).start()
    pl.semaphore_wait(pltpu.get_barrier_semaphore(), count - 1)

    for a in range(heads_here):
        def send_in(d, carry, a=a):
            for t in range(3):
                inward(t, a, peer(d), me).start()
            return carry

        lax.fori_loop(1, count, send_in, 0)
        for t in range(3):
            own_in(t, a).start()

    for a in range(heads_here):
        for t in range(3):
            own_in(t, a).wait()

        def arrive(d, carry, a=a):
            for t in range(3):
                inward(t, a, me, peer(d)).wait_recv()
            return carry

        lax.fori_loop(1, count, arrive, 0)
        own_list(a).wait()

        def one(i, a=a):
            ids = [lists[a, i * entries + e] for e in range(entries)]
            far_out[a][i] = attend_tile(ids, far_in[a][2, i], far_in[a])

        def work(d, carry, a=a, one=one):
            one(peer(d))

            @pl.when(d > 1)
            def _():
                outward(a, peer(d - 1), me).start()

            return carry

        lax.fori_loop(1, count + 1, work, 0)
        own_out(a).start()

    for a in range(heads_here):
        own_out(a).wait()

        def finish(d, carry, a=a):
            for t in range(3):
                inward(t, a, peer(d), me).wait_send()
            outward(a, peer(d), me).wait_send()
            outward(a, me, peer(d)).wait_recv()
            return carry

        lax.fori_loop(1, count, finish, 0)


def general_exchange(sizes, collective_id, block_lists, table, keys, values, queries):
    count = sizes[0] * sizes[1] * sizes[2]
    rows = keys.shape[0]
    stage = jnp.stack([keys, values, queries]).reshape(3, rows, HEADS, HEAD_DIM)
    stage = jnp.swapaxes(stage, 1, 2)
    block = (rows, HEAD_DIM)
    heads_here = HEADS // count
    list_rows = block_lists.reshape(HEADS, -1)
    anywhere = pl.BlockSpec(memory_space=pl.ANY)
    dma = pltpu.SemaphoreType.DMA
    scratch = [pltpu.SMEM((heads_here, list_rows.shape[1]), jnp.int32), dma((heads_here,))]
    scratch += [pltpu.VMEM((3, count) + block, jnp.bfloat16)] * heads_here
    scratch += [pltpu.VMEM((count,) + block, jnp.bfloat16)] * heads_here
    scratch += [dma((4, heads_here, count))] * 2 + [dma((4, heads_here))]
    landed = pl.pallas_call(
        functools.partial(general_kernel, sizes, block_lists.shape[2]),
        out_shape=jax.ShapeDtypeStruct((HEADS,) + block, jnp.bfloat16),
        in_specs=[anywhere, anywhere],
        out_specs=anywhere,
        scratch_shapes=scratch,
        compiler_params=pltpu.CompilerParams(
            collective_id=collective_id, has_side_effects=True
        ),
    )(stage, list_rows)
    return jnp.swapaxes(landed, 0, 1).reshape(rows, HEADS * HEAD_DIM)


def split_kernel(sizes, near, table_ref, k_all, v_hbm, q_hbm, out_ref, table, v_all, q_all, by_head, stage, near_in, near_side,
                 near_out, far_in, far_out, landed, local_sem, below_sem, above_sem, near_send, near_recv, near_back,
                 hop_send, hop_recv, help_send, far_send, far_recv, far_back):
    n_blk, n_head, n_sub = sizes
    line_count = n_head * n_sub
    far = HEADS - near
    near_slots = -(-near // line_count)
    far_slots = -(-far // n_blk)
    score_scale = 1.0 / math.sqrt(HEAD_DIM)

    blk, sub = lax.axis_index("blk"), lax.axis_index("sub")
    line = lax.axis_index("head") * n_sub + sub
    first = blk * line_count

    def near_number(a, target_line):
        return a * line_count + target_line % n_sub * n_head + target_line // n_sub

    def far_number(a, target_blk):
        mirrored = target_blk + sub % 2 * (n_blk - 1 - 2 * target_blk)
        return a * n_blk + (mirrored + n_blk - 1) % n_blk

    def line_peer(d):
        return (line + d) % line_count

    def blk_peer(d):
        return (blk + d) % n_blk

    def if_near(a, target_line, action):
        pl.when(near_number(a, target_line) < near)(action)

    def if_far(a, target_blk, action):
        pl.when(far_number(a, target_blk) < far)(action)

    def each_other(count, peer, test, action):
        def one(d, carry):
            test(peer(d), lambda: action(peer(d)))
            return carry

        lax.fori_loop(1, count, one, 0)

    def other_far(a, action):
        each_other(n_blk, blk_peer, functools.partial(if_far, a), action)

    def other_near(a, action):
        each_other(line_count, line_peer, functools.partial(if_near, a), action)

    def take(sem, unit, pieces):
        if pieces:
            part = unit.at[pl.ds(0, pieces)]
            pltpu.make_async_copy(part, part, sem).wait()

    def take_others(sem, unit, a, own, total, count):
        rest = total % count
        if total >= count:
            pl.when(a < total // count)(lambda: take(sem, unit, count - 1))
        if rest:
            last = a == total // count
            pl.when(jnp.logical_and(last, own < total))(lambda: take(sem, unit, rest - 1))
            pl.when(jnp.logical_and(last, own >= total))(lambda: take(sem, unit, rest))

    def take_far(sem, unit, a):
        take_others(sem, unit, a, far_number(a, blk), far, n_blk)

    def take_near(sem, unit, a):
        take_others(sem, unit, a, near_number(a, line), near, line_count)

    def near_inward(a, t, target):
        return remote_copy(
            sizes, stage.at[near_number(a, target), t], near_in.at[a, line, t],
            near_send.at[a], near_recv.at[a], first + target,
        )

    def near_outward(a, target):
        return remote_copy(
            sizes, near_out.at[a, target], landed.at[near_number(a, line)],
            near_send.at[a], near_back.at[a], first + target,
        )

    def hop(a, direction):
        step = 1 - 2 * direction
        return remote_copy(
            sizes, near_in.at[a, :, pl.ds(0, 2)], near_side.at[a, direction],
            hop_send.at[a, direction], hop_recv.at[a, direction],
            (blk + n_blk + step) % n_blk * line_count + line,
        )

    def each_hop(action, sending):
        up, down = blk < n_blk - 1, blk > 0
        pl.when(up if sending else down)(functools.partial(action, 0))
        pl.when(down if sending else up)(functools.partial(action, 1))

    rest = near % line_count
    shared = n_head == 2 and rest % 2 == 1
    shared_slot, shared_line = near // line_count, rest // 2

    def shared_hop(direction):
        step = 1 - 2 * direction
        here = pl.ds(0, n_sub)
        return remote_copy(
            sizes, near_in.at[shared_slot, here, pl.ds(0, 2)],
            near_side.at[shared_slot, direction, here],
            hop_send.at[shared_slot, direction], hop_recv.at[shared_slot, direction],
            (blk + n_blk + step) % n_blk * line_count + line,
        )

    def helping_hop(direction):
        step = 1 - 2 * direction
        return remote_copy(
            sizes, stage.at[near - 1, pl.ds(0, 2)], near_side.at[shared_slot, direction, line],
            help_send.at[direction], hop_recv.at[shared_slot, direction],
            (blk + n_blk + step) % n_blk * line_count + shared_line,
        )

    def own_hops(a, action):
        if shared:
            split = jnp.logical_and(a == shared_slot, line == shared_line)
            pl.when(split)(lambda: each_hop(lambda d: action(shared_hop(d)), True))
            pl.when(jnp.logical_not(split))(lambda: each_hop(lambda d: action(hop(a, d)), True))
        else:
            each_hop(lambda d: action(hop(a, d)), True)

    def help_hops(action):
        if shared:
            pl.when(line >= n_sub)(lambda: each_hop(lambda d: action(helping_hop(d)), True))

    def far_inward(a, t, target):
        return remote_copy(
            sizes, stage.at[near + far_number(a, target), t], far_in.at[a, blk, t],
            far_send.at[a], far_recv.at[a], target * line_count + line,
        )

    def far_outward(a, target):
        return remote_copy(
            sizes, far_out.at[a, target], landed.at[near + far_number(a, blk)],
            far_send.at[a], far_back.at[a], target * line_count + line,
        )

    last = n_blk - 1
    below, above = (blk > 0).astype(jnp.int32), (blk < last).astype(jnp.int32)
    pl.when(blk < last)(lambda: greet(sizes, first + line_count + line))
    pl.when(blk > 0)(lambda: greet(sizes, first - line_count + line))
    for d in range(1, line_count):
        greet(sizes, first + line_peer(d))
    loads = [
        pltpu.make_async_copy(table_ref, table, local_sem.at[0]),
        pltpu.make_async_copy(v_hbm, v_all, local_sem.at[1]),
        pltpu.make_async_copy(q_hbm, q_all, local_sem.at[2]),
    ]
    for load in loads:
        load.start()

    def clear(side):
        def clear_tile(i, carry):
            near_side[i // line_count, side, i % line_count] = jnp.zeros(
                near_side.shape[3:], near_side.dtype
            )
            return carry

        lax.fori_loop(0, near_slots * line_count, clear_tile, 0)

    def columns(h):
        return pl.ds(pl.multiple_of(h * HEAD_DIM, HEAD_DIM), HEAD_DIM)

    def split_heads(t, source):
        def split_head(h, carry):
            by_head[t, h] = source[:, columns(h)]
            return carry

        lax.fori_loop(0, HEADS, split_head, 0)

    def tell(step, sem):
        pl.semaphore_signal(
            sem, inc=1,
            device_id=rank_of(first + step * line_count + line, n_head, n_sub),
            device_id_type=pl.DeviceIdType.MESH,
        )

    def pass_on(step, sem):
        def heard(e, carry):
            pl.semaphore_wait(sem, 1)
            pl.when(blk < last if step > 0 else blk > 0)(lambda: tell(step, sem))
            return carry

        known = blk if step > 0 else last - blk
        lax.fori_loop(0, jnp.maximum(known - 1, 0), heard, 0)

    def stage_far(a, t):
        def own():
            far_in[a, blk, t] = by_head[t, table[0, near + far_number(a, blk)]]

        def other(target):
            slot = near + far_number(a, target)
            stage[slot, t] = by_head[t, table[0, slot]]

        other_far(a, other)
        if_far(a, blk, own)

    def stage_near(a, t):
        def own():
            near_in[a, line, t] = by_head[t, table[0, near_number(a, line)]]

        def other(target):
            slot = near_number(a, target)
            stage[slot, t] = by_head[t, table[0, slot]]

        other_near(a, other)
        if_near(a, line, own)

    def send_far(t, beside):
        def one(a, carry):
            def other(target):
                next_to = jnp.abs(target - blk) == 1
                pl.when(next_to if beside else jnp.logical_not(next_to))(
                    lambda: far_inward(a, t, target).start()
                )

            other_far(a, other)
            return carry

        lax.fori_loop(0, far_slots, one, 0)

    def send_near(t):
        def one(a, carry):
            other_near(a, lambda target: near_inward(a, t, target).start())
            return carry

        lax.fori_loop(0, near_slots, one, 0)

    def each_slot(slots, action, t):
        def one(a, carry):
            action(a, t)
            return carry

        lax.fori_loop(0, slots, one, 0)

    def tensor(t, carry):
        @pl.when(t == 0)
        def _():
            split_heads(0, k_all)
            loads[0].wait()

        @pl.when(t == 1)
        def _():
            loads[1].wait()
            split_heads(1, v_all)

        @pl.when(t == 2)
        def _():
            loads[2].wait()
            split_heads(2, q_all)

        each_slot(far_slots, stage_far, t)

        @pl.when(t == 0)
        def _():
            pl.semaphore_wait(
                pltpu.get_barrier_semaphore(), line_count - 1 + below + above
            )

            @pl.when(jnp.logical_and(blk > 0, blk < last))
            def _():
                tell(1, below_sem)
                tell(-1, above_sem)

        send_far(t, True)
        each_slot(near_slots, stage_near, t)
        send_near(t)

        @pl.when(t == 0)
        def _():
            pl.when(blk == 0)(functools.partial(clear, 0))
            pl.when(blk == last)(functools.partial(clear, 1))
            pass_on(1, below_sem)
            pass_on(-1, above_sem)

        send_far(t, False)
        return carry

    lax.fori_loop(0, 3, tensor, 0)

    def near_whole(a, carry):
        def whole():
            take(near_recv.at[a], near_in.at[a], line_count - 1)
            own_hops(a, lambda copy: copy.start())

        if_near(a, line, whole)
        return carry

    lax.fori_loop(0, near_slots, near_whole, 0)
    help_hops(lambda copy: copy.start())

    def attend_pair(query, bits, tiles):
        rows = query.shape[0] // len(bits)
        scores = [[] for _ in bits]
        for e in range(0, len(tiles), 2):
            some = tiles[e : e + 2]
            s = lax.dot_general(
                query, jnp.concatenate([tile[0]() for tile in some]), (((1,), (1,)), ((), ())),
                preferred_element_type=jnp.float32,
            ) * score_scale
            for half, mask in enumerate(bits):
                for c, (_, _, place) in enumerate(some):
                    part = s[half * rows : (half + 1) * rows, c * rows : (c + 1) * rows]
                    bias = jnp.where((mask >> place) % 2 == 1, 0.0, NEG_FLOOR)
                    scores[half].append(part + bias)
        tops = [
            jnp.max(functools.reduce(jnp.maximum, part), axis=1, keepdims=True) for part in scores
        ]
        totals, accum = [None] * len(bits), None
        for e in range(0, len(tiles), 2):
            some, weights = tiles[e : e + 2], []
            for half, top in enumerate(tops):
                wide = [jnp.exp(scores[half][e + c] - top) for c in range(len(some))]
                for w in wide:
                    totals[half] = w if totals[half] is None else totals[half] + w
                weights.append(jnp.concatenate([w.astype(jnp.bfloat16) for w in wide], axis=1))
            part = jnp.dot(
                jnp.concatenate(weights), jnp.concatenate([tile[1]() for tile in some]),
                preferred_element_type=jnp.float32,
            )
            accum = part if accum is None else accum + part
        return [
            (
                accum[half * rows : (half + 1) * rows] / jnp.sum(total, axis=1, keepdims=True)
            ).astype(jnp.bfloat16)
            for half, total in enumerate(totals)
        ]

    def pick(ref, c):
        return lambda: ref[c, 0], lambda: ref[c, 1]

    def far_pair(a, sources):
        number = near + far_number(a, blk)
        bits = [table[8 + source * line_count + line, number] for source in sources]
        query = jnp.concatenate([far_in[a, source, 2] for source in sources])
        held = far_in.at[a]
        return attend_pair(
            query, bits, [pick(held, c) + (c * line_count + line,) for c in range(n_blk)]
        )

    def near_pair(a, sources):
        number = near_number(a, line)
        bits = [table[8 + first + source, number] * (1 << line_count) for source in sources]
        query = jnp.concatenate([near_in[a, source, 2] for source in sources])
        tiles = []
        for f, held in ((1, near_in.at[a]), (0, near_side.at[a, 0]), (2, near_side.at[a, 1])):
            tiles += [
                pick(held, c) + (first + f * line_count + c,) for c in range(line_count)
            ]
        return attend_pair(query, bits, tiles)

    def work_through(a, count, peer, pair, outs, number, outward):
        def work(i, carry):
            d = 2 * i + 1
            results = pair(a, (peer(d), peer(d + 1)))

            @pl.when(i > 0)
            def _():
                outward(a, peer(d - 2)).start()
                outward(a, peer(d - 1)).start()

            outs[a, peer(d)] = results[0]

            @pl.when(d + 1 < count)
            def _():
                outs[a, peer(d + 1)] = results[1]

            @pl.when(d + 1 == count)
            def _():
                landed[number] = results[1]

            return carry

        lax.fori_loop(0, count // 2, work, 0)
        outward(a, peer(count - 1)).start()

    def far_work(a, carry):
        take_far(far_send.at[a], far_in.at[a], a)

        def whole():
            take(far_recv.at[a], far_in.at[a], n_blk - 1)
            work_through(
                a, n_blk, blk_peer, far_pair, far_out, near + far_number(a, blk), far_outward
            )

        if_far(a, blk, whole)
        return carry

    lax.fori_loop(0, far_slots, far_work, 0)

    def near_work(a, carry):
        take_near(near_send.at[a], near_in.at[a], a)

        def whole():
            each_hop(lambda direction: hop(a, direction).wait_recv(), False)
            work_through(
                a, line_count, line_peer, near_pair, near_out, near_number(a, line), near_outward
            )

        if_near(a, line, whole)
        return carry

    lax.fori_loop(0, near_slots, near_work, 0)

    def finish_near(a, carry):
        def own():
            take(near_send.at[a], near_out.at[a], line_count - 1)
            own_hops(a, lambda copy: copy.wait_send())

        if_near(a, line, own)
        take_near(near_back.at[a], near_out.at[a], a)
        return carry

    def finish_far(a, carry):
        if_far(a, blk, lambda: take(far_send.at[a], far_out.at[a], n_blk - 1))
        take_far(far_back.at[a], far_out.at[a], a)
        return carry

    lax.fori_loop(0, near_slots, finish_near, 0)
    help_hops(lambda copy: copy.wait_send())
    lax.fori_loop(0, far_slots, finish_far, 0)

    def restore(i, carry):
        for e in range(4):
            h = i * 4 + e
            out_ref[:, columns(h)] = landed[table[1, h]]
        return carry

    lax.fori_loop(0, HEADS // 4, restore, 0)


def split_exchange(sizes, near, collective_id, block_lists, table, keys, values, queries):
    n_blk, line_count = sizes[0], sizes[1] * sizes[2]
    rows, width = keys.shape
    near_slots = -(-near // line_count)
    far_slots = -(-(HEADS - near) // n_blk)
    block = (rows, HEAD_DIM)
    vmem = pl.BlockSpec(memory_space=pltpu.VMEM)
    anywhere = pl.BlockSpec(memory_space=pl.ANY)
    dma = pltpu.SemaphoreType.DMA

    def buffer(*lead):
        return pltpu.VMEM(lead + block, jnp.bfloat16)

    return pl.pallas_call(
        functools.partial(split_kernel, sizes, near),
        out_shape=jax.ShapeDtypeStruct((rows, width), jnp.bfloat16),
        in_specs=[anywhere, vmem, anywhere, anywhere],
        out_specs=vmem,
        scratch_shapes=[
            pltpu.SMEM(table.shape, jnp.int32),
            pltpu.VMEM((rows, width), jnp.bfloat16),
            pltpu.VMEM((rows, width), jnp.bfloat16),
            buffer(3, HEADS),
            buffer(HEADS, 3),
            buffer(near_slots, line_count, 3),
            buffer(near_slots, 2, line_count, 2),
            buffer(near_slots, line_count),
            buffer(far_slots, n_blk, 3),
            buffer(far_slots, n_blk),
            buffer(HEADS),
            dma((3,)),
            pltpu.SemaphoreType.REGULAR,
            pltpu.SemaphoreType.REGULAR,
            dma((near_slots,)),
            dma((near_slots,)),
            dma((near_slots,)),
            dma((near_slots, 2)),
            dma((near_slots, 2)),
            dma((2,)),
            dma((far_slots,)),
            dma((far_slots,)),
            dma((far_slots,)),
        ],
        compiler_params=pltpu.CompilerParams(
            collective_id=collective_id, has_side_effects=True
        ),
    )(table, keys, values, queries)


def sort_kernel(frames, line_count, entries, lists_hbm, k_hbm, table, choice, k_all, lists_ref,
                sems):
    lists_load = pltpu.make_async_copy(lists_hbm, lists_ref, sems.at[0])
    load = pltpu.make_async_copy(k_hbm, k_all, sems.at[1])
    lists_load.start()
    load.start()
    lists_load.wait()
    ids = lists_ref[...]
    steps, heads = ids.shape
    tiles = steps // entries
    per_frame = steps // frames
    away = None
    for f in range(frames):
        part = ids[f * per_frame : (f + 1) * per_frame]
        outside = jnp.logical_or(part < (f - 1) * line_count, part >= (f + 2) * line_count)
        found = jnp.max(jnp.where(outside, 1, 0), axis=0, keepdims=True)
        away = found if away is None else jnp.maximum(away, found)
    row = lax.broadcasted_iota(jnp.int32, (heads, heads), 0)
    col = lax.broadcasted_iota(jnp.int32, (heads, heads), 1)
    away_col = jnp.broadcast_to(away, (heads, heads))
    away_row = jnp.broadcast_to(
        jnp.sum(jnp.where(row == col, away_col, 0), axis=1, keepdims=True), (heads, heads)
    )
    same = away_row == away_col
    ahead = jnp.where(same, jnp.where(row < col, 1, 0), away_col)
    place = jnp.sum(ahead, axis=0, keepdims=True)
    behind = jnp.where(same, jnp.where(col < row, 1, 0), away_row)
    place_of_row = jnp.sum(behind, axis=1, keepdims=True)
    perm = jnp.sum(
        jnp.where(jnp.broadcast_to(place_of_row, (heads, heads)) == col, row, 0),
        axis=0, keepdims=True,
    )
    table[0:1, 0:heads] = perm
    table[1:2, 0:heads] = place
    bits = None
    for e in range(entries):
        bit = jnp.left_shift(1, lists_ref[pl.ds(e, tiles, stride=entries), :])
        bits = bit if bits is None else jnp.bitwise_or(bits, bit)
    picks = jnp.where(jnp.broadcast_to(place, (heads, heads)) == row, 1.0, 0.0).astype(jnp.bfloat16)
    low, high = [
        lax.dot_general(
            part.astype(jnp.float32).astype(jnp.bfloat16), picks, (((1,), (1,)), ((), ())),
            preferred_element_type=jnp.float32,
        ).astype(jnp.int32)
        for part in (jnp.bitwise_and(bits, 255), jnp.right_shift(bits, 8))
    ]
    table[8 : 8 + tiles, 0:heads] = low + high * 256
    near = heads - jnp.sum(away.astype(jnp.float32)).astype(jnp.int32)
    least, most = EXACT_COUNTS[0], EXACT_COUNTS[-1]
    known = jnp.logical_and(near >= least, near <= most)
    choice[0] = jnp.where(known, near - least, most - least + 1)
    load.wait()


def sort_heads(line_count, keys, block_lists):
    heads, tiles, entries = block_lists.shape
    by_row = jnp.transpose(block_lists, (1, 2, 0)).reshape(tiles * entries, heads)
    vmem = pl.BlockSpec(memory_space=pltpu.VMEM)
    return pl.pallas_call(
        functools.partial(sort_kernel, tiles // line_count, line_count, entries),
        out_shape=(
            jax.ShapeDtypeStruct((8 + tiles, 128), jnp.int32),
            jax.ShapeDtypeStruct((1,), jnp.int32),
            jax.ShapeDtypeStruct(keys.shape, jnp.bfloat16),
        ),
        in_specs=[pl.BlockSpec(memory_space=pl.ANY)] * 2,
        out_specs=(vmem, pl.BlockSpec(memory_space=pltpu.SMEM), vmem),
        scratch_shapes=[pltpu.VMEM(by_row.shape, jnp.int32), pltpu.SemaphoreType.DMA((2,))],
    )(by_row, keys)


def solution(mesh):
    sizes = tuple(mesh.shape[axis] for axis in ("blk", "head", "sub"))
    line_count = sizes[1] * sizes[2]
    count = sizes[0] * line_count

    def body(queries, keys, values, block_lists):
        fits = queries.shape[0] == TILE and HEADS % count == 0 and count <= 16 and sizes[0] % 2 == 0 and line_count % 2 == 0
        if not fits or block_lists.shape[1] != count:
            return per_device(queries, keys, values, block_lists)
        table, choice, held = sort_heads(line_count, keys, block_lists)
        branches = [
            functools.partial(split_exchange, sizes, n, number)
            for number, n in enumerate(EXACT_COUNTS)
        ]
        branches.append(functools.partial(general_exchange, sizes, len(EXACT_COUNTS)))
        return lax.switch(choice[0], branches, block_lists, table, held, values, queries)

    spec = P(("grp", "blk", "head", "sub"), None)
    return jax.shard_map(
        body, mesh=mesh, in_specs=(spec, spec, spec, P()), out_specs=spec, check_vma=False
    )
```

```python
import functools
import math

import jax
import jax.numpy as jnp
from jax import lax
from jax.experimental import pallas as pl
from jax.experimental.pallas import tpu as pltpu
from jax.sharding import PartitionSpec as P

HEADS = 32
HEAD_DIM = 128
TILE = 128


NEG_FLOOR = -1e30


def query_rows(block_lists, first_head, heads_here, query_tokens):
    tile_ids = jnp.arange(block_lists.shape[1], dtype=jnp.int32)
    lists_local = lax.dynamic_slice_in_dim(block_lists, first_head, heads_here, 0)
    tile_mask = jnp.any(lists_local[:, :, :, None] == tile_ids, axis=2).astype(jnp.bfloat16)
    query_onehot = ((query_tokens // TILE)[:, None] == tile_ids[None, :]).astype(jnp.bfloat16)
    listed = jnp.einsum("qi,hij->hqj", query_onehot, tile_mask, preferred_element_type=jnp.float32)
    return listed.astype(jnp.bfloat16)


def attend_block(state_now, key_block, value_block, allowed, query_local, score_scale):
    top_old, total_old, accum_old = state_now
    scores = (
        jnp.einsum("qhd,khd->hqk", query_local, key_block, preferred_element_type=jnp.float32)
        * score_scale
    )
    top_new = jnp.maximum(top_old, jnp.max(jnp.where(allowed, scores, NEG_FLOOR), axis=2))
    factor = jnp.exp(top_old - top_new)
    weights = jnp.where(allowed, jnp.exp(scores - top_new[:, :, None]), 0.0)
    total_new = total_old * factor + jnp.sum(weights, axis=2)
    product = jnp.einsum(
        "hqk,khd->qhd",
        weights.astype(jnp.bfloat16),
        value_block,
        preferred_element_type=jnp.float32,
    )
    accum_new = accum_old * jnp.transpose(factor)[:, :, None] + product
    return (top_new, total_new, accum_new)


def make_step(query_local, listed_rows, key_token, block_len, tile_total):
    score_scale = 1.0 / math.sqrt(HEAD_DIM)
    tile_ids = jnp.arange(tile_total, dtype=jnp.int32)

    def fold_step(state_now, piece, first_row):
        key_piece, value_piece = piece
        block_count = key_piece.shape[0] // block_len

        def one_block(block_index, state_in):
            key_block = lax.dynamic_slice_in_dim(key_piece, block_index * block_len, block_len, 0)
            value_block = lax.dynamic_slice_in_dim(
                value_piece, block_index * block_len, block_len, 0
            )
            positions = block_index * block_len + jnp.arange(block_len, dtype=jnp.int32)
            key_tiles = key_token(positions) // TILE
            key_onehot = (tile_ids[:, None] == key_tiles[None, :]).astype(jnp.bfloat16)
            allowed = (
                jnp.einsum(
                    "hqj,jk->hqk", listed_rows, key_onehot, preferred_element_type=jnp.float32
                )
                > 0.5
            )
            result = attend_block(
                state_in, key_block, value_block, allowed, query_local, score_scale
            )
            return result

        return lax.fori_loop(0, block_count, one_block, state_now)

    return fold_step


def start_state(heads_here, block_len):
    top_all = jnp.full((heads_here, block_len), NEG_FLOOR, jnp.float32)
    total_all = jnp.zeros((heads_here, block_len), jnp.float32)
    accum_all = jnp.zeros((block_len, heads_here, HEAD_DIM), jnp.float32)
    return (top_all, total_all, accum_all)


def normalize(state_end):
    top_all, total_all, accum_all = state_end
    return (accum_all / jnp.transpose(total_all)[:, :, None]).astype(jnp.bfloat16)


def per_device(queries, keys, values, block_lists):
    row_count, col_count = queries.shape
    n_head = lax.axis_size("head")
    n_sub = lax.axis_size("sub")
    blk_index = lax.axis_index("blk")
    head_index = lax.axis_index("head")
    sub_index = lax.axis_index("sub")
    tile_total = block_lists.shape[1]
    heads_here = HEADS // (n_head * n_sub)
    block_len = row_count * n_head * n_sub

    def inward(tensor):
        return tensor.reshape(1, 1, row_count, n_head, n_sub, heads_here * HEAD_DIM)

    query_six, keys_six, values_six = (
        lax.all_to_all(
            lax.all_to_all(inward(queries), "head", split_axis=3, concat_axis=1, tiled=True),
            "sub",
            split_axis=4,
            concat_axis=0,
            tiled=True,
        ),
        lax.all_to_all(
            lax.all_to_all(inward(keys), "head", split_axis=3, concat_axis=1, tiled=True),
            "sub",
            split_axis=4,
            concat_axis=0,
            tiled=True,
        ),
        lax.all_to_all(
            lax.all_to_all(inward(values), "head", split_axis=3, concat_axis=1, tiled=True),
            "sub",
            split_axis=4,
            concat_axis=0,
            tiled=True,
        ),
    )
    query_local = query_six.reshape(block_len, heads_here, HEAD_DIM)
    keys_local = keys_six.reshape(block_len, heads_here, HEAD_DIM)
    values_local = values_six.reshape(block_len, heads_here, HEAD_DIM)

    def key_token(positions):
        source_dev = positions // block_len
        within = positions % block_len
        sub_source = within // (n_head * row_count)
        head_source = within // row_count % n_head
        offset = within % row_count
        return ((source_dev * n_head + head_source) * n_sub + sub_source) * row_count + offset

    query_tokens = key_token(blk_index * block_len + jnp.arange(block_len, dtype=jnp.int32))
    first_head = (head_index * n_sub + sub_index) * heads_here
    listed_rows = query_rows(block_lists, first_head, heads_here, query_tokens)
    fold_step = make_step(query_local, listed_rows, key_token, block_len, tile_total)
    state_end = fold_step(
        start_state(heads_here, block_len),
        (
            lax.all_gather(keys_local, "blk", axis=0, tiled=True),
            lax.all_gather(values_local, "blk", axis=0, tiled=True),
        ),
        jnp.int32(0),
    )
    result_rows = normalize(state_end)
    attended = result_rows.reshape(n_sub, n_head, row_count, 1, 1, heads_here * HEAD_DIM)
    returned = lax.all_to_all(
        lax.all_to_all(attended, "head", split_axis=1, concat_axis=3, tiled=True),
        "sub",
        split_axis=0,
        concat_axis=4,
        tiled=True,
    )
    return returned.reshape(row_count, col_count)


EXACT_COUNTS = tuple(range(10, 23))


def rank_of(rank, n_head, n_sub):
    line_count = n_head * n_sub
    return {
        "blk": rank // line_count,
        "head": rank // n_sub % n_head,
        "sub": rank % n_sub,
    }


def remote_copy(sizes, src, dst, send, recv, rank):
    return pltpu.make_async_remote_copy(
        src_ref=src,
        dst_ref=dst,
        send_sem=send,
        recv_sem=recv,
        device_id=rank_of(rank, sizes[1], sizes[2]),
        device_id_type=pl.DeviceIdType.MESH,
    )


def greet(sizes, rank):
    pl.semaphore_signal(
        pltpu.get_barrier_semaphore(), inc=1,
        device_id=rank_of(rank, sizes[1], sizes[2]),
        device_id_type=pl.DeviceIdType.MESH,
    )


def attend_tile(ids, query, buf):
    score_scale = 1.0 / math.sqrt(HEAD_DIM)
    scores, top = [], None
    for tile in ids:
        s = lax.dot_general(
            query, buf[0, tile], (((1,), (1,)), ((), ())), preferred_element_type=jnp.float32
        ) * score_scale
        scores.append(s)
        top = s if top is None else jnp.maximum(top, s)
    row_top = jnp.max(top, axis=1, keepdims=True)
    total, accum = None, None
    for e, tile in enumerate(ids):
        w = jnp.exp(scores[e] - row_top)
        if e:
            repeat = tile == ids[0]
            for f in range(1, e):
                repeat = jnp.logical_or(repeat, tile == ids[f])
            w = w * jnp.where(repeat, 0.0, 1.0)
        part = jnp.dot(
            w.astype(jnp.bfloat16), buf[1, tile], preferred_element_type=jnp.float32
        )
        total = w if total is None else total + w
        accum = part if accum is None else accum + part
    row_total = jnp.sum(total, axis=1, keepdims=True)
    return (accum / row_total).astype(jnp.bfloat16)


def general_kernel(sizes, entries, stage, list_rows, landed, lists, list_sem, *scratch):
    n_blk, n_head, n_sub = sizes
    line_count = n_head * n_sub
    count = n_blk * line_count
    heads_here = HEADS // count
    far_in = scratch[:heads_here]
    far_out = scratch[heads_here : 2 * heads_here]
    send_sem, recv_sem, local_sem = scratch[2 * heads_here :]
    line = lax.axis_index("head") * n_sub + lax.axis_index("sub")
    me = lax.axis_index("blk") * line_count + line

    def peer(d):
        return (me + d) % count

    def inward(t, a, target, sender):
        return remote_copy(
            sizes, stage.at[t, a * count + target], far_in[a].at[t, sender],
            send_sem.at[t, a, target], recv_sem.at[t, a, sender], target,
        )

    def outward(a, target, sender):
        return remote_copy(
            sizes, far_out[a].at[target], landed.at[a * count + sender],
            send_sem.at[3, a, target], recv_sem.at[3, a, sender], target,
        )

    def own_in(t, a):
        return pltpu.make_async_copy(
            stage.at[t, a * count + me], far_in[a].at[t, me], local_sem.at[t, a]
        )

    def own_out(a):
        return pltpu.make_async_copy(
            far_out[a].at[me], landed.at[a * count + me], local_sem.at[3, a]
        )

    def own_list(a):
        return pltpu.make_async_copy(
            list_rows.at[a * count + me], lists.at[a], list_sem.at[a]
        )

    def greet_all(d, carry):
        greet(sizes, peer(d))
        return carry

    lax.fori_loop(1, count, greet_all, 0)
    for a in range(heads_here):
        own_list(a).start()
    pl.semaphore_wait(pltpu.get_barrier_semaphore(), count - 1)

    for a in range(heads_here):
        def send_in(d, carry, a=a):
            for t in range(3):
                inward(t, a, peer(d), me).start()
            return carry

        lax.fori_loop(1, count, send_in, 0)
        for t in range(3):
            own_in(t, a).start()

    for a in range(heads_here):
        for t in range(3):
            own_in(t, a).wait()

        def arrive(d, carry, a=a):
            for t in range(3):
                inward(t, a, me, peer(d)).wait_recv()
            return carry

        lax.fori_loop(1, count, arrive, 0)
        own_list(a).wait()

        def one(i, a=a):
            ids = [lists[a, i * entries + e] for e in range(entries)]
            far_out[a][i] = attend_tile(ids, far_in[a][2, i], far_in[a])

        def work(d, carry, a=a, one=one):
            one(peer(d))

            @pl.when(d > 1)
            def _():
                outward(a, peer(d - 1), me).start()

            return carry

        lax.fori_loop(1, count + 1, work, 0)
        own_out(a).start()

    for a in range(heads_here):
        own_out(a).wait()

        def finish(d, carry, a=a):
            for t in range(3):
                inward(t, a, peer(d), me).wait_send()
            outward(a, peer(d), me).wait_send()
            outward(a, me, peer(d)).wait_recv()
            return carry

        lax.fori_loop(1, count, finish, 0)


def general_exchange(sizes, collective_id, block_lists, table, keys, values, queries):
    count = sizes[0] * sizes[1] * sizes[2]
    rows = keys.shape[0]
    stage = jnp.stack([keys, values, queries]).reshape(3, rows, HEADS, HEAD_DIM)
    stage = jnp.swapaxes(stage, 1, 2)
    block = (rows, HEAD_DIM)
    heads_here = HEADS // count
    list_rows = block_lists.reshape(HEADS, -1)
    anywhere = pl.BlockSpec(memory_space=pl.ANY)
    dma = pltpu.SemaphoreType.DMA
    scratch = [pltpu.SMEM((heads_here, list_rows.shape[1]), jnp.int32), dma((heads_here,))]
    scratch += [pltpu.VMEM((3, count) + block, jnp.bfloat16)] * heads_here
    scratch += [pltpu.VMEM((count,) + block, jnp.bfloat16)] * heads_here
    scratch += [dma((4, heads_here, count))] * 2 + [dma((4, heads_here))]
    landed = pl.pallas_call(
        functools.partial(general_kernel, sizes, block_lists.shape[2]),
        out_shape=jax.ShapeDtypeStruct((HEADS,) + block, jnp.bfloat16),
        in_specs=[anywhere, anywhere],
        out_specs=anywhere,
        scratch_shapes=scratch,
        compiler_params=pltpu.CompilerParams(
            collective_id=collective_id, has_side_effects=True
        ),
    )(stage, list_rows)
    return jnp.swapaxes(landed, 0, 1).reshape(rows, HEADS * HEAD_DIM)


def split_kernel(sizes, near, table_ref, k_all, v_hbm, q_hbm, out_ref, table, v_all, q_all, by_head, stage, near_in, near_side,
                 near_out, far_in, far_out, landed, local_sem, below_sem, above_sem, near_send, near_recv, near_back,
                 hop_send, hop_recv, help_send, far_send, far_recv, far_back):
    n_blk, n_head, n_sub = sizes
    line_count = n_head * n_sub
    far = HEADS - near
    near_slots = -(-near // line_count)
    far_slots = -(-far // n_blk)
    score_scale = 1.0 / math.sqrt(HEAD_DIM)

    blk, sub = lax.axis_index("blk"), lax.axis_index("sub")
    line = lax.axis_index("head") * n_sub + sub
    first = blk * line_count

    def near_number(a, target_line):
        return a * line_count + target_line % n_sub * n_head + target_line // n_sub

    def far_number(a, target_blk):
        mirrored = target_blk + sub % 2 * (n_blk - 1 - 2 * target_blk)
        return a * n_blk + (mirrored + n_blk - 1) % n_blk

    def line_peer(d):
        return (line + d) % line_count

    def blk_peer(d):
        return (blk + d) % n_blk

    def if_near(a, target_line, action):
        pl.when(near_number(a, target_line) < near)(action)

    def if_far(a, target_blk, action):
        pl.when(far_number(a, target_blk) < far)(action)

    def each_other(count, peer, test, action):
        def one(d, carry):
            test(peer(d), lambda: action(peer(d)))
            return carry

        lax.fori_loop(1, count, one, 0)

    def other_far(a, action):
        each_other(n_blk, blk_peer, functools.partial(if_far, a), action)

    def other_near(a, action):
        each_other(line_count, line_peer, functools.partial(if_near, a), action)

    def take(sem, unit, pieces):
        if pieces:
            part = unit.at[pl.ds(0, pieces)]
            pltpu.make_async_copy(part, part, sem).wait()

    def take_others(sem, unit, a, own, total, count):
        rest = total % count
        if total >= count:
            pl.when(a < total // count)(lambda: take(sem, unit, count - 1))
        if rest:
            last = a == total // count
            pl.when(jnp.logical_and(last, own < total))(lambda: take(sem, unit, rest - 1))
            pl.when(jnp.logical_and(last, own >= total))(lambda: take(sem, unit, rest))

    def take_far(sem, unit, a):
        take_others(sem, unit, a, far_number(a, blk), far, n_blk)

    def take_near(sem, unit, a):
        take_others(sem, unit, a, near_number(a, line), near, line_count)

    def near_inward(a, t, target):
        return remote_copy(
            sizes, stage.at[near_number(a, target), t], near_in.at[a, line, t],
            near_send.at[a], near_recv.at[a], first + target,
        )

    def near_outward(a, target):
        return remote_copy(
            sizes, near_out.at[a, target], landed.at[near_number(a, line)],
            near_send.at[a], near_back.at[a], first + target,
        )

    def hop(a, direction):
        step = 1 - 2 * direction
        return remote_copy(
            sizes, near_in.at[a, :, pl.ds(0, 2)], near_side.at[a, direction],
            hop_send.at[a, direction], hop_recv.at[a, direction],
            (blk + n_blk + step) % n_blk * line_count + line,
        )

    def each_hop(action, sending):
        up, down = blk < n_blk - 1, blk > 0
        pl.when(up if sending else down)(functools.partial(action, 0))
        pl.when(down if sending else up)(functools.partial(action, 1))

    rest = near % line_count
    shared = n_head == 2 and rest % 2 == 1
    shared_slot, shared_line = near // line_count, rest // 2

    def shared_hop(direction):
        step = 1 - 2 * direction
        here = pl.ds(0, n_sub)
        return remote_copy(
            sizes, near_in.at[shared_slot, here, pl.ds(0, 2)],
            near_side.at[shared_slot, direction, here],
            hop_send.at[shared_slot, direction], hop_recv.at[shared_slot, direction],
            (blk + n_blk + step) % n_blk * line_count + line,
        )

    def helping_hop(direction):
        step = 1 - 2 * direction
        return remote_copy(
            sizes, stage.at[near - 1, pl.ds(0, 2)], near_side.at[shared_slot, direction, line],
            help_send.at[direction], hop_recv.at[shared_slot, direction],
            (blk + n_blk + step) % n_blk * line_count + shared_line,
        )

    def own_hops(a, action):
        if shared:
            split = jnp.logical_and(a == shared_slot, line == shared_line)
            pl.when(split)(lambda: each_hop(lambda d: action(shared_hop(d)), True))
            pl.when(jnp.logical_not(split))(lambda: each_hop(lambda d: action(hop(a, d)), True))
        else:
            each_hop(lambda d: action(hop(a, d)), True)

    def help_hops(action):
        if shared:
            pl.when(line >= n_sub)(lambda: each_hop(lambda d: action(helping_hop(d)), True))

    def far_inward(a, t, target):
        return remote_copy(
            sizes, stage.at[near + far_number(a, target), t], far_in.at[a, blk, t],
            far_send.at[a], far_recv.at[a], target * line_count + line,
        )

    def far_outward(a, target):
        return remote_copy(
            sizes, far_out.at[a, target], landed.at[near + far_number(a, blk)],
            far_send.at[a], far_back.at[a], target * line_count + line,
        )

    last = n_blk - 1
    below, above = (blk > 0).astype(jnp.int32), (blk < last).astype(jnp.int32)
    pl.when(blk < last)(lambda: greet(sizes, first + line_count + line))
    pl.when(blk > 0)(lambda: greet(sizes, first - line_count + line))
    for d in range(1, line_count):
        greet(sizes, first + line_peer(d))
    loads = [
        pltpu.make_async_copy(table_ref, table, local_sem.at[0]),
        pltpu.make_async_copy(v_hbm, v_all, local_sem.at[1]),
        pltpu.make_async_copy(q_hbm, q_all, local_sem.at[2]),
    ]
    for load in loads:
        load.start()

    def clear(side):
        def clear_tile(i, carry):
            near_side[i // line_count, side, i % line_count] = jnp.zeros(
                near_side.shape[3:], near_side.dtype
            )
            return carry

        lax.fori_loop(0, near_slots * line_count, clear_tile, 0)

    def columns(h):
        return pl.ds(pl.multiple_of(h * HEAD_DIM, HEAD_DIM), HEAD_DIM)

    def split_heads(t, source):
        def split_head(h, carry):
            by_head[t, h] = source[:, columns(h)]
            return carry

        lax.fori_loop(0, HEADS, split_head, 0)

    def tell(step, sem):
        pl.semaphore_signal(
            sem, inc=1,
            device_id=rank_of(first + step * line_count + line, n_head, n_sub),
            device_id_type=pl.DeviceIdType.MESH,
        )

    def pass_on(step, sem):
        def heard(e, carry):
            pl.semaphore_wait(sem, 1)
            pl.when(blk < last if step > 0 else blk > 0)(lambda: tell(step, sem))
            return carry

        known = blk if step > 0 else last - blk
        lax.fori_loop(0, jnp.maximum(known - 1, 0), heard, 0)

    def stage_far(a, t):
        def own():
            far_in[a, blk, t] = by_head[t, table[0, near + far_number(a, blk)]]

        def other(target):
            slot = near + far_number(a, target)
            stage[slot, t] = by_head[t, table[0, slot]]

        other_far(a, other)
        if_far(a, blk, own)

    def stage_near(a, t):
        def own():
            near_in[a, line, t] = by_head[t, table[0, near_number(a, line)]]

        def other(target):
            slot = near_number(a, target)
            stage[slot, t] = by_head[t, table[0, slot]]

        other_near(a, other)
        if_near(a, line, own)

    def send_far(t, beside):
        def one(a, carry):
            def other(target):
                next_to = jnp.abs(target - blk) == 1
                pl.when(next_to if beside else jnp.logical_not(next_to))(
                    lambda: far_inward(a, t, target).start()
                )

            other_far(a, other)
            return carry

        lax.fori_loop(0, far_slots, one, 0)

    def send_near(t):
        def one(a, carry):
            other_near(a, lambda target: near_inward(a, t, target).start())
            return carry

        lax.fori_loop(0, near_slots, one, 0)

    def each_slot(slots, action, t):
        def one(a, carry):
            action(a, t)
            return carry

        lax.fori_loop(0, slots, one, 0)

    def tensor(t, carry):
        @pl.when(t == 0)
        def _():
            split_heads(0, k_all)
            loads[0].wait()

        @pl.when(t == 1)
        def _():
            loads[1].wait()
            split_heads(1, v_all)

        @pl.when(t == 2)
        def _():
            loads[2].wait()
            split_heads(2, q_all)

        each_slot(far_slots, stage_far, t)

        @pl.when(t == 0)
        def _():
            pl.semaphore_wait(
                pltpu.get_barrier_semaphore(), line_count - 1 + below + above
            )

            @pl.when(jnp.logical_and(blk > 0, blk < last))
            def _():
                tell(1, below_sem)
                tell(-1, above_sem)

        send_far(t, True)
        each_slot(near_slots, stage_near, t)
        send_near(t)
        return carry

    lax.fori_loop(0, 3, tensor, 0)
    pass_on(1, below_sem)
    pass_on(-1, above_sem)

    def send_rest(t, carry):
        send_far(t, False)
        return carry

    lax.fori_loop(0, 3, send_rest, 0)
    pl.when(blk == 0)(functools.partial(clear, 0))
    pl.when(blk == last)(functools.partial(clear, 1))

    def near_whole(a, carry):
        def whole():
            take(near_recv.at[a], near_in.at[a], line_count - 1)
            own_hops(a, lambda copy: copy.start())

        if_near(a, line, whole)
        return carry

    lax.fori_loop(0, near_slots, near_whole, 0)
    help_hops(lambda copy: copy.start())

    def attend_pair(query, bits, tiles):
        rows = query.shape[0] // len(bits)
        scores = [[] for _ in bits]
        for e in range(0, len(tiles), 2):
            some = tiles[e : e + 2]
            s = lax.dot_general(
                query, jnp.concatenate([tile[0]() for tile in some]), (((1,), (1,)), ((), ())),
                preferred_element_type=jnp.float32,
            ) * score_scale
            for half, mask in enumerate(bits):
                for c, (_, _, place) in enumerate(some):
                    part = s[half * rows : (half + 1) * rows, c * rows : (c + 1) * rows]
                    bias = jnp.where((mask >> place) % 2 == 1, 0.0, NEG_FLOOR)
                    scores[half].append(part + bias)
        tops = [
            jnp.max(functools.reduce(jnp.maximum, part), axis=1, keepdims=True) for part in scores
        ]
        totals, accum = [None] * len(bits), None
        for e in range(0, len(tiles), 2):
            some, weights = tiles[e : e + 2], []
            for half, top in enumerate(tops):
                wide = [jnp.exp(scores[half][e + c] - top) for c in range(len(some))]
                for w in wide:
                    totals[half] = w if totals[half] is None else totals[half] + w
                weights.append(jnp.concatenate([w.astype(jnp.bfloat16) for w in wide], axis=1))
            part = jnp.dot(
                jnp.concatenate(weights), jnp.concatenate([tile[1]() for tile in some]),
                preferred_element_type=jnp.float32,
            )
            accum = part if accum is None else accum + part
        return [
            (
                accum[half * rows : (half + 1) * rows] / jnp.sum(total, axis=1, keepdims=True)
            ).astype(jnp.bfloat16)
            for half, total in enumerate(totals)
        ]

    def pick(ref, c):
        return lambda: ref[c, 0], lambda: ref[c, 1]

    def far_pair(a, sources):
        number = near + far_number(a, blk)
        bits = [table[8 + source * line_count + line, number] for source in sources]
        query = jnp.concatenate([far_in[a, source, 2] for source in sources])
        held = far_in.at[a]
        return attend_pair(
            query, bits, [pick(held, c) + (c * line_count + line,) for c in range(n_blk)]
        )

    def near_pair(a, sources):
        number = near_number(a, line)
        bits = [table[8 + first + source, number] * (1 << line_count) for source in sources]
        query = jnp.concatenate([near_in[a, source, 2] for source in sources])
        tiles = []
        for f, held in ((1, near_in.at[a]), (0, near_side.at[a, 0]), (2, near_side.at[a, 1])):
            tiles += [
                pick(held, c) + (first + f * line_count + c,) for c in range(line_count)
            ]
        return attend_pair(query, bits, tiles)

    def work_through(a, count, peer, pair, outs, number, outward):
        def work(i, carry):
            d = 2 * i + 1
            results = pair(a, (peer(d), peer(d + 1)))

            @pl.when(i > 0)
            def _():
                outward(a, peer(d - 2)).start()
                outward(a, peer(d - 1)).start()

            outs[a, peer(d)] = results[0]

            @pl.when(d + 1 < count)
            def _():
                outs[a, peer(d + 1)] = results[1]

            @pl.when(d + 1 == count)
            def _():
                landed[number] = results[1]

            return carry

        lax.fori_loop(0, count // 2, work, 0)
        outward(a, peer(count - 1)).start()

    def far_work(a, carry):
        take_far(far_send.at[a], far_in.at[a], a)

        def whole():
            take(far_recv.at[a], far_in.at[a], n_blk - 1)
            work_through(
                a, n_blk, blk_peer, far_pair, far_out, near + far_number(a, blk), far_outward
            )

        if_far(a, blk, whole)
        return carry

    lax.fori_loop(0, far_slots, far_work, 0)

    def near_work(a, carry):
        take_near(near_send.at[a], near_in.at[a], a)

        def whole():
            each_hop(lambda direction: hop(a, direction).wait_recv(), False)
            work_through(
                a, line_count, line_peer, near_pair, near_out, near_number(a, line), near_outward
            )

        if_near(a, line, whole)
        return carry

    lax.fori_loop(0, near_slots, near_work, 0)

    def finish_near(a, carry):
        def own():
            take(near_send.at[a], near_out.at[a], line_count - 1)
            own_hops(a, lambda copy: copy.wait_send())

        if_near(a, line, own)
        take_near(near_back.at[a], near_out.at[a], a)
        return carry

    def finish_far(a, carry):
        if_far(a, blk, lambda: take(far_send.at[a], far_out.at[a], n_blk - 1))
        take_far(far_back.at[a], far_out.at[a], a)
        return carry

    lax.fori_loop(0, near_slots, finish_near, 0)
    help_hops(lambda copy: copy.wait_send())
    lax.fori_loop(0, far_slots, finish_far, 0)

    def restore(i, carry):
        for e in range(4):
            h = i * 4 + e
            out_ref[:, columns(h)] = landed[table[1, h]]
        return carry

    lax.fori_loop(0, HEADS // 4, restore, 0)


def split_exchange(sizes, near, collective_id, block_lists, table, keys, values, queries):
    n_blk, line_count = sizes[0], sizes[1] * sizes[2]
    rows, width = keys.shape
    near_slots = -(-near // line_count)
    far_slots = -(-(HEADS - near) // n_blk)
    block = (rows, HEAD_DIM)
    vmem = pl.BlockSpec(memory_space=pltpu.VMEM)
    anywhere = pl.BlockSpec(memory_space=pl.ANY)
    dma = pltpu.SemaphoreType.DMA

    def buffer(*lead):
        return pltpu.VMEM(lead + block, jnp.bfloat16)

    return pl.pallas_call(
        functools.partial(split_kernel, sizes, near),
        out_shape=jax.ShapeDtypeStruct((rows, width), jnp.bfloat16),
        in_specs=[anywhere, vmem, anywhere, anywhere],
        out_specs=vmem,
        scratch_shapes=[
            pltpu.SMEM(table.shape, jnp.int32),
            pltpu.VMEM((rows, width), jnp.bfloat16),
            pltpu.VMEM((rows, width), jnp.bfloat16),
            buffer(3, HEADS),
            buffer(HEADS, 3),
            buffer(near_slots, line_count, 3),
            buffer(near_slots, 2, line_count, 2),
            buffer(near_slots, line_count),
            buffer(far_slots, n_blk, 3),
            buffer(far_slots, n_blk),
            buffer(HEADS),
            dma((3,)),
            pltpu.SemaphoreType.REGULAR,
            pltpu.SemaphoreType.REGULAR,
            dma((near_slots,)),
            dma((near_slots,)),
            dma((near_slots,)),
            dma((near_slots, 2)),
            dma((near_slots, 2)),
            dma((2,)),
            dma((far_slots,)),
            dma((far_slots,)),
            dma((far_slots,)),
        ],
        compiler_params=pltpu.CompilerParams(
            collective_id=collective_id, has_side_effects=True
        ),
    )(table, keys, values, queries)


def sort_kernel(frames, line_count, entries, lists_hbm, k_hbm, table, choice, k_all, lists_ref,
                sems):
    lists_load = pltpu.make_async_copy(lists_hbm, lists_ref, sems.at[0])
    load = pltpu.make_async_copy(k_hbm, k_all, sems.at[1])
    lists_load.start()
    load.start()
    lists_load.wait()
    ids = lists_ref[...]
    steps, heads = ids.shape
    tiles = steps // entries
    per_frame = steps // frames
    away = None
    for f in range(frames):
        part = ids[f * per_frame : (f + 1) * per_frame]
        outside = jnp.logical_or(part < (f - 1) * line_count, part >= (f + 2) * line_count)
        found = jnp.max(jnp.where(outside, 1, 0), axis=0, keepdims=True)
        away = found if away is None else jnp.maximum(away, found)
    row = lax.broadcasted_iota(jnp.int32, (heads, heads), 0)
    col = lax.broadcasted_iota(jnp.int32, (heads, heads), 1)
    away_col = jnp.broadcast_to(away, (heads, heads))
    away_row = jnp.broadcast_to(
        jnp.sum(jnp.where(row == col, away_col, 0), axis=1, keepdims=True), (heads, heads)
    )
    same = away_row == away_col
    ahead = jnp.where(same, jnp.where(row < col, 1, 0), away_col)
    place = jnp.sum(ahead, axis=0, keepdims=True)
    behind = jnp.where(same, jnp.where(col < row, 1, 0), away_row)
    place_of_row = jnp.sum(behind, axis=1, keepdims=True)
    perm = jnp.sum(
        jnp.where(jnp.broadcast_to(place_of_row, (heads, heads)) == col, row, 0),
        axis=0, keepdims=True,
    )
    table[0:1, 0:heads] = perm
    table[1:2, 0:heads] = place
    bits = None
    for e in range(entries):
        bit = jnp.left_shift(1, lists_ref[pl.ds(e, tiles, stride=entries), :])
        bits = bit if bits is None else jnp.bitwise_or(bits, bit)
    picks = jnp.where(jnp.broadcast_to(place, (heads, heads)) == row, 1.0, 0.0).astype(jnp.bfloat16)
    low, high = [
        lax.dot_general(
            part.astype(jnp.float32).astype(jnp.bfloat16), picks, (((1,), (1,)), ((), ())),
            preferred_element_type=jnp.float32,
        ).astype(jnp.int32)
        for part in (jnp.bitwise_and(bits, 255), jnp.right_shift(bits, 8))
    ]
    table[8 : 8 + tiles, 0:heads] = low + high * 256
    near = heads - jnp.sum(away.astype(jnp.float32)).astype(jnp.int32)
    least, most = EXACT_COUNTS[0], EXACT_COUNTS[-1]
    known = jnp.logical_and(near >= least, near <= most)
    choice[0] = jnp.where(known, near - least, most - least + 1)
    load.wait()


def sort_heads(line_count, keys, block_lists):
    heads, tiles, entries = block_lists.shape
    by_row = jnp.transpose(block_lists, (1, 2, 0)).reshape(tiles * entries, heads)
    vmem = pl.BlockSpec(memory_space=pltpu.VMEM)
    return pl.pallas_call(
        functools.partial(sort_kernel, tiles // line_count, line_count, entries),
        out_shape=(
            jax.ShapeDtypeStruct((8 + tiles, 128), jnp.int32),
            jax.ShapeDtypeStruct((1,), jnp.int32),
            jax.ShapeDtypeStruct(keys.shape, jnp.bfloat16),
        ),
        in_specs=[pl.BlockSpec(memory_space=pl.ANY)] * 2,
        out_specs=(vmem, pl.BlockSpec(memory_space=pltpu.SMEM), vmem),
        scratch_shapes=[pltpu.VMEM(by_row.shape, jnp.int32), pltpu.SemaphoreType.DMA((2,))],
    )(by_row, keys)


def solution(mesh):
    sizes = tuple(mesh.shape[axis] for axis in ("blk", "head", "sub"))
    line_count = sizes[1] * sizes[2]
    count = sizes[0] * line_count

    def body(queries, keys, values, block_lists):
        fits = queries.shape[0] == TILE and HEADS % count == 0 and count <= 16 and sizes[0] % 2 == 0 and line_count % 2 == 0
        if not fits or block_lists.shape[1] != count:
            return per_device(queries, keys, values, block_lists)
        table, choice, held = sort_heads(line_count, keys, block_lists)
        branches = [
            functools.partial(split_exchange, sizes, n, number)
            for number, n in enumerate(EXACT_COUNTS)
        ]
        branches.append(functools.partial(general_exchange, sizes, len(EXACT_COUNTS)))
        return lax.switch(choice[0], branches, block_lists, table, held, values, queries)

    spec = P(("grp", "blk", "head", "sub"), None)
    return jax.shard_map(
        body, mesh=mesh, in_specs=(spec, spec, spec, P()), out_specs=spec, check_vma=False
    )
```
